512 devices in a mesh: shard: 128 (over z, x, core), tensor: 4 (over y).
Axes of the slice: x: 4, y: 4, z: 16, core: 2. Of those that a mesh axis runs over, the one named last changes fastest.
Arguments:
- grads: bfloat16 [128, 4, 1536, 1024], P('shard', None, None, 'tensor'), may hold values from -240 to 240
- master: float32 [1536, 1024], P('shard', 'tensor'), may hold values from -3 to 3
- moment1: float32 [1536, 1024], P('shard', 'tensor'), may hold values from -3 to 3
- moment2: float32 [1536, 1024], P('shard', 'tensor'), may hold values from 0.25 to 1
- ema: float32 [1536, 1024], P('shard', 'tensor'), may hold values from -3 to 3
Outputs:
- new_master: float32 [1536, 1024], P('shard', 'tensor')
- new_moment1: float32 [1536, 1024], P('shard', 'tensor')
- new_moment2: float32 [1536, 1024], P('shard', 'tensor')
- new_ema: float32 [1536, 1024], P('shard', 'tensor')
- weights: bfloat16 [1536, 1024], P(None, 'tensor')
The draws below stay inside these ranges and needn't reach their ends.
All inputs are finite; a program needn't handle non-finite values.
Results may differ from the reference program's by a relative error of at most 0.0004.
Values may be sent and summed in bfloat16 or wider, within the bound.
No kernel may reach another device: no remote copies, remote signals or barrier semaphores. Data moves between devices by JAX's collectives and lax.ppermute only.
A program may use at most 64 MiB of HBM per device.

```python
import math
import jax
import jax.numpy as jnp
from jax import lax

D = 1536
MICRO = 4
STEP = 10
COLS = 1024
ELEMS = 1572864
N_SHARD = 128


def draw_grads(key, part):
    keys = jax.random.split(key, 3)
    shape = (N_SHARD, MICRO, D, COLS)
    rows = jnp.arange(D, dtype=jnp.float32) / D
    base = jnp.clip(jax.random.normal(keys[0], shape, jnp.float32), -6.0, 6.0)
    row_scale = 10.0 ** rows
    col_scale = jnp.exp(jax.random.uniform(keys[1], (COLS,), jnp.float32) * jnp.log(10.0))
    paired = jax.random.permutation(keys[2], N_SHARD)
    block = jnp.arange(D) // (D // N_SHARD)
    spike = jnp.where(block[None, :] == paired[:, None], 4.0, 1.0)
    values = 0.1 * base * row_scale[None, None, :, None] * col_scale[None, None, None, :] * spike[:, None, :, None]
    return values.astype(jnp.bfloat16)


def block_levels(stream_key, extent, cuts, low, high):
    loudness = 1.0
    for dim, shards_of in cuts:
        heights = jax.random.uniform(jax.random.fold_in(jax.random.fold_in(stream_key, 6), dim), (shards_of,), jnp.float32, low / len(cuts), high / len(cuts))
        loudness = loudness * jnp.repeat(jnp.exp(heights), extent[dim] // shards_of).reshape((-1,) + (1,) * (len(extent) - 1 - dim))
    return loudness


def gaussian(key, dims, width, most, cuts=(), kind=jnp.bfloat16):
    entries = jax.random.normal(key, dims, jnp.float32) * width
    if len(cuts) > 0:
        entries = block_levels(key, dims, cuts, -0.22, 0.18) * entries
    return jnp.clip(entries, min=-most, max=most).astype(kind)


def setup_inputs(seed: int = 0) -> dict:
    seeds = jax.random.split(jax.random.key(seed), 6)
    return {
        "grads": draw_grads(jax.random.fold_in(seeds[5], 71), 0),
        "master": gaussian(seeds[1], (D, COLS), 0.5, 3.0, ((0, 128), (1, 4)), jnp.float32),
        "moment1": gaussian(seeds[2], (D, COLS), 0.5, 3.0, ((0, 128), (1, 4)), jnp.float32),
        "moment2": jnp.clip(jnp.exp(math.log(1.0) - 1.3862944 * jax.random.uniform(seeds[3], (D, COLS), jnp.float32) ** block_levels(seeds[3], (D, COLS), ((0, 128), (1, 4)), -0.2, 0.2)), 0.25, 1.0),
        "ema": gaussian(seeds[4], (D, COLS), 0.5, 3.0, ((0, 128), (1, 4)), jnp.float32),
    }


def reference(grads, master, moment1, moment2, ema):

    def add_replica(carry, piece):
        return (carry + lax.optimization_barrier(jnp.sum(piece.astype(jnp.float32), axis=0)), None)
    total, unused = lax.scan(add_replica, jnp.zeros((D, COLS), jnp.float32), grads)
    sq = jnp.sum(total * total)
    scale = jnp.minimum(1.0, 1.0 / jnp.sqrt(sq / ELEMS + 1e-06))
    clipped = scale * total
    new_moment1 = 0.9 * moment1 + 0.1 * clipped
    new_moment2 = 0.95 * moment2 + 0.05 * clipped * clipped
    first_hat = new_moment1 / (1.0 - 0.9 ** STEP)
    second_hat = new_moment2 / (1.0 - 0.95 ** STEP)
    new_master = master - 0.02 * (first_hat / (jnp.sqrt(second_hat) + 1e-08) + 0.1 * master)
    new_ema = 0.99 * ema + 0.01 * new_master
    weights = new_master.astype(jnp.bfloat16)
    return (new_master, new_moment1, new_moment2, new_ema, weights)
```

```python
import jax
import jax.numpy as jnp
from jax import lax
from jax.experimental import pallas as pl
from jax.experimental.pallas import tpu as pltpu
from jax.sharding import Mesh, PartitionSpec as P

STEP = 10
BETA_ONE = 0.9
BETA_TWO = 0.95
LEARN_RATE = 0.02
DECAY_WEIGHT = 0.1
EMA_KEEP = 0.99

Z, X, C, T = 16, 4, 2, 4
ROWS, COLS = 12, 256
PR, PC = 24, 128

F32 = jnp.float32
BF16 = jnp.bfloat16


def to_piece(v):
    return jnp.concatenate([v[0:8, :PC], v[0:8, PC:], v[8:12, :PC], v[8:12, PC:]], axis=0)


def from_piece(p):
    top = jnp.concatenate([p[0:8], p[8:16]], axis=1)
    low = jnp.concatenate([p[16:20], p[20:24]], axis=1)
    return jnp.concatenate([top, low], axis=0)


def sum_kernel(g_ref, o_ref):
    for zz in range(g_ref.shape[1] // (X * C * ROWS)):
        for pair in range(X // 2):
            at = zz * X * C * ROWS + pair * 48
            v = g_ref[0, at : at + 48, :].astype(F32)
            for m in range(1, g_ref.shape[0]):
                v = v + g_ref[m, at : at + 48, :].astype(F32)
            for k in range(4):
                o_ref[k % 2, pair * 2 + k // 2, zz] = to_piece(v[k * ROWS : (k + 1) * ROWS])


def micro_sum(local):
    steps = 4
    zs = Z // steps
    return pl.pallas_call(
        sum_kernel,
        out_shape=jax.ShapeDtypeStruct((C, X, Z, PR, PC), F32),
        grid=(steps,),
        in_specs=[pl.BlockSpec((local.shape[0], zs * X * C * ROWS, COLS), lambda i: (0, i, 0))],
        out_specs=pl.BlockSpec((C, X, zs, PR, PC), lambda i: (0, 0, i, 0, 0)),
        name="micro_sum",
    )(local)


def total_kernel(p_ref, t_ref, s_ref):
    t = jnp.sum(p_ref[...], axis=0)
    t_ref[...] = from_piece(t)
    sq = t * t
    part = sq[0:8] + sq[8:16] + sq[16:24]
    s_ref[...] = jnp.broadcast_to(part[None], s_ref.shape)


def spread_kernel(p_ref, s_ref):
    s_ref[...] = jnp.broadcast_to(jnp.sum(p_ref[...], axis=0)[None], s_ref.shape)


def update_kernel(elements, sq_ref, t_ref, ma_ref, m1_ref, m2_ref, em_ref, oma, om1, om2, oem, ow):
    sq = jnp.sum(jnp.sum(sq_ref[...], axis=0))
    sq = jnp.full((1, COLS), sq, F32)
    scale = jnp.minimum(1.0, 1.0 / jnp.sqrt(sq / elements + 1e-06))
    clipped = scale * t_ref[...]
    master = ma_ref[...]
    m1 = BETA_ONE * m1_ref[...] + (1.0 - BETA_ONE) * clipped
    m2 = BETA_TWO * m2_ref[...] + (1.0 - BETA_TWO) * clipped * clipped
    first_hat = m1 / (1.0 - BETA_ONE**STEP)
    second_hat = m2 / (1.0 - BETA_TWO**STEP)
    new = master - LEARN_RATE * (
        first_hat / (jnp.sqrt(second_hat) + 1e-08) + DECAY_WEIGHT * master
    )
    oma[...] = new
    om1[...] = m1
    om2[...] = m2
    oem[...] = EMA_KEEP * em_ref[...] + (1.0 - EMA_KEEP) * new
    ow[...] = jnp.broadcast_to(to_piece(new).astype(BF16)[None], ow.shape)


def place_kernel(w_ref, o_ref):
    for zz in range(w_ref.shape[2]):
        for pair in range(X // 2):
            parts = [
                from_piece(w_ref[k % 2, pair * 2 + k // 2, zz].astype(F32)) for k in range(4)
            ]
            at = zz * X * C * ROWS + pair * 48
            o_ref[at : at + 48, :] = jnp.concatenate(parts, axis=0).astype(BF16)


def place(w):
    steps = 4
    zs = Z // steps
    return pl.pallas_call(
        place_kernel,
        out_shape=jax.ShapeDtypeStruct((C * X * Z * ROWS, COLS), BF16),
        grid=(steps,),
        in_specs=[pl.BlockSpec((C, X, zs, PR, PC), lambda i: (0, 0, i, 0, 0))],
        out_specs=pl.BlockSpec((zs * X * C * ROWS, COLS), lambda i: (i, 0)),
        name="place",
    )(w)


def exchange(v, axes):
    return lax.all_to_all(v, axes, split_axis=0, concat_axis=0, tiled=True)


def shards(grads, master, moment1, moment2, ema):
    local = grads[0]
    elements = local.shape[1] * local.shape[2] * T

    part = micro_sum(local)
    part = jnp.sum(exchange(part, "c"), axis=0)
    part = jnp.sum(exchange(part, "x"), axis=0)
    part = exchange(part, "z")
    total, sq = pl.pallas_call(
        total_kernel,
        out_shape=(
            jax.ShapeDtypeStruct((ROWS, COLS), F32),
            jax.ShapeDtypeStruct((X * C * T, 8, 128), F32),
        ),
        name="total",
    )(part)
    sq = exchange(sq, ("x", "c", "t"))
    sq = pl.pallas_call(
        spread_kernel, out_shape=jax.ShapeDtypeStruct((Z, 8, 128), F32), name="spread"
    )(sq)
    sq = exchange(sq, "z")

    state = jax.ShapeDtypeStruct((ROWS, COLS), F32)
    new_master, new_moment1, new_moment2, new_ema, w = pl.pallas_call(
        lambda *refs: update_kernel(elements, *refs),
        out_shape=(state, state, state, state, jax.ShapeDtypeStruct((Z, PR, PC), BF16)),
        name="update",
    )(sq, total, master, moment1, moment2, ema)

    w = exchange(w, "z")
    w = exchange(jnp.broadcast_to(w[None], (X,) + w.shape), "x")
    w = lax.all_gather(w, "c", axis=0, tiled=False)
    weights = place(w)
    return (new_master, new_moment1, new_moment2, new_ema, weights)


def solution(mesh):
    fine = Mesh(mesh.devices.reshape(Z, X, C, T), ("z", "x", "c", "t"))
    rows = ("z", "x", "c")
    return jax.shard_map(
        shards,
        mesh=fine,
        in_specs=(P(rows, None, None, "t"),) + (P(rows, "t"),) * 4,
        out_specs=(P(rows, "t"),) * 4 + (P(None, "t"),),
        check_vma=False,
    )
```

```python
import jax
import jax.numpy as jnp
from jax import lax
from jax.experimental import pallas as pl
from jax.experimental.pallas import tpu as pltpu
from jax.sharding import Mesh, PartitionSpec as P

STEP = 10
BETA_ONE = 0.9
BETA_TWO = 0.95
LEARN_RATE = 0.02
DECAY_WEIGHT = 0.1
EMA_KEEP = 0.99

ZH, ZL, X, C, T = 4, 4, 4, 2, 4
ROWS, COLS = 12, 256
PR, PC = 24, 128
SET = ZH * PR

F32 = jnp.float32
BF16 = jnp.bfloat16


def to_piece(v):
    return jnp.concatenate([v[0:8, :PC], v[0:8, PC:], v[8:12, :PC], v[8:12, PC:]], axis=0)


def from_piece(p):
    top = jnp.concatenate([p[0:8], p[8:16]], axis=1)
    low = jnp.concatenate([p[16:20], p[20:24]], axis=1)
    return jnp.concatenate([top, low], axis=0)


def sum_kernel(g_ref, o_ref):
    for zl in range(ZL):
        for pair in range(X // 2):
            at = zl * X * C * ROWS + pair * 48
            v = g_ref[0, at : at + 48, :].astype(F32)
            for m in range(1, g_ref.shape[0]):
                v = v + g_ref[m, at : at + 48, :].astype(F32)
            for k in range(4):
                o_ref[k % 2, pair * 2 + k // 2, zl, 0] = to_piece(v[k * ROWS : (k + 1) * ROWS])


def micro_sum(local):
    rows = ZL * X * C * ROWS
    return pl.pallas_call(
        sum_kernel,
        out_shape=jax.ShapeDtypeStruct((C, X, ZL, ZH, PR, PC), F32),
        grid=(ZH,),
        in_specs=[pl.BlockSpec((local.shape[0], rows, COLS), lambda i: (0, i, 0))],
        out_specs=pl.BlockSpec((C, X, ZL, 1, PR, PC), lambda i: (0, 0, 0, i, 0, 0)),
        name="micro_sum",
    )(local)


def pack_kernel(p_ref, ma_ref, m1_ref, m2_ref, o_ref):
    part = jnp.sum(p_ref[...], axis=0)
    state = [to_piece(r[...]) for r in (ma_ref, m1_ref, m2_ref)]
    o_ref[...] = jnp.broadcast_to(jnp.concatenate([part] + state, axis=0)[None], o_ref.shape)


def total_kernel(p_ref, t_ref, s_ref):
    t = jnp.sum(p_ref[:, :SET, :], axis=0)
    t_ref[...] = t
    sq = t * t
    s_ref[...] = jnp.broadcast_to(jnp.sum(sq.reshape(-1, 8, PC), axis=0)[None], s_ref.shape)


def adam(scale, total, master, moment1, moment2):
    clipped = scale * total
    m1 = BETA_ONE * moment1 + (1.0 - BETA_ONE) * clipped
    m2 = BETA_TWO * moment2 + (1.0 - BETA_TWO) * clipped * clipped
    first_hat = m1 / (1.0 - BETA_ONE**STEP)
    second_hat = m2 / (1.0 - BETA_TWO**STEP)
    new = master - LEARN_RATE * (
        first_hat / (jnp.sqrt(second_hat) + 1e-08) + DECAY_WEIGHT * master
    )
    return new, m1, m2


def update_kernel(elements, sq_ref, t_ref, p_ref, ma_ref, m1_ref, m2_ref, em_ref, oma, om1, om2, oem, ow):
    sq = jnp.sum(jnp.sum(sq_ref[...], axis=0))
    sq = jnp.full((1, PC), sq, F32)
    scale = jnp.minimum(1.0, 1.0 / jnp.sqrt(sq / elements + 1e-06))
    for k in range(ZH):
        state = [p_ref[k, SET + j * PR : SET + (j + 1) * PR, :] for j in range(3)]
        new, _, _ = adam(scale, t_ref[k * PR : (k + 1) * PR, :], *state)
        ow[:, k] = jnp.broadcast_to(new.astype(BF16)[None], (ow.shape[0], PR, PC))
    at = pl.multiple_of(lax.axis_index("zh") * PR, 8)
    total = from_piece(t_ref[pl.ds(at, PR), :])
    wide = jnp.concatenate([scale, scale], axis=1)
    new, m1, m2 = adam(wide, total, ma_ref[...], m1_ref[...], m2_ref[...])
    oma[...] = new
    om1[...] = m1
    om2[...] = m2
    oem[...] = EMA_KEEP * em_ref[...] + (1.0 - EMA_KEEP) * new


def place_kernel(w_ref, o_ref):
    for zl in range(ZL):
        for pair in range(X // 2):
            parts = [
                from_piece(w_ref[k % 2, pair * 2 + k // 2, zl, 0].astype(F32)) for k in range(4)
            ]
            at = zl * X * C * ROWS + pair * 48
            o_ref[at : at + 48, :] = jnp.concatenate(parts, axis=0).astype(BF16)


def place(w):
    rows = ZL * X * C * ROWS
    return pl.pallas_call(
        place_kernel,
        out_shape=jax.ShapeDtypeStruct((ZH * rows, COLS), BF16),
        grid=(ZH,),
        in_specs=[pl.BlockSpec((C, X, ZL, 1, PR, PC), lambda i: (0, 0, 0, i, 0, 0))],
        out_specs=pl.BlockSpec((rows, COLS), lambda i: (i, 0)),
        name="place",
    )(w)


def exchange(v, axes):
    return lax.all_to_all(v, axes, split_axis=0, concat_axis=0, tiled=True)


def copies(v, n):
    return jnp.broadcast_to(v[None], (n,) + v.shape)


def shards(grads, master, moment1, moment2, ema):
    local = grads[0]
    elements = local.shape[1] * local.shape[2] * T

    part = micro_sum(local)
    part = jnp.sum(exchange(part, "c"), axis=0)
    part = jnp.sum(exchange(part, "x"), axis=0)
    part = exchange(part.reshape(ZL, SET, PC), "zl")
    both = pl.pallas_call(
        pack_kernel,
        out_shape=jax.ShapeDtypeStruct((ZH, SET + 3 * PR, PC), F32),
        name="pack",
    )(part, master, moment1, moment2)
    both = exchange(both, "zh")
    total, sq = pl.pallas_call(
        total_kernel,
        out_shape=(
            jax.ShapeDtypeStruct((SET, PC), F32),
            jax.ShapeDtypeStruct((X * C * T, 8, PC), F32),
        ),
        name="total",
    )(both)
    sq = jnp.sum(exchange(sq, ("x", "c", "t")), axis=0)
    sq = exchange(copies(sq, ZL), "zl")

    state = jax.ShapeDtypeStruct((ROWS, COLS), F32)
    new_master, new_moment1, new_moment2, new_ema, w = pl.pallas_call(
        lambda *refs: update_kernel(elements, *refs),
        out_shape=(state, state, state, state, jax.ShapeDtypeStruct((ZL, ZH, PR, PC), BF16)),
        name="update",
    )(sq, total, both, master, moment1, moment2, ema)

    w = exchange(w, "zl")
    w = exchange(copies(w, X), "x")
    w = lax.all_gather(w, "c", axis=0, tiled=False)
    weights = place(w)
    return (new_master, new_moment1, new_moment2, new_ema, weights)


def solution(mesh):
    fine = Mesh(mesh.devices.reshape(ZH, ZL, X, C, T), ("zh", "zl", "x", "c", "t"))
    rows = ("zh", "zl", "x", "c")
    return jax.shard_map(
        shards,
        mesh=fine,
        in_specs=(P(rows, None, None, "t"),) + (P(rows, "t"),) * 4,
        out_specs=(P(rows, "t"),) * 4 + (P(None, "t"),),
        check_vma=False,
    )
```

```python
import jax
import jax.numpy as jnp
from jax import lax
from jax.experimental import pallas as pl
from jax.experimental.pallas import tpu as pltpu
from jax.sharding import Mesh, PartitionSpec as P

STEP = 10
BETA_ONE = 0.9
BETA_TWO = 0.95
LEARN_RATE = 0.02
DECAY_WEIGHT = 0.1
EMA_KEEP = 0.99

ZH, ZL, X, C, T = 4, 4, 4, 2, 4
ROWS, COLS = 12, 256
PR, PC = 24, 128

F32 = jnp.float32
BF16 = jnp.bfloat16


def to_piece(v):
    return jnp.concatenate([v[0:8, :PC], v[0:8, PC:], v[8:12, :PC], v[8:12, PC:]], axis=0)


def from_piece(p):
    top = jnp.concatenate([p[0:8], p[8:16]], axis=1)
    low = jnp.concatenate([p[16:20], p[20:24]], axis=1)
    return jnp.concatenate([top, low], axis=0)


def sum_kernel(g_ref, ma_ref, m1_ref, m2_ref, o_ref, st_ref):
    for zl in range(ZL):
        for pair in range(X // 2):
            at = zl * X * C * ROWS + pair * 48
            v = g_ref[0, at : at + 48, :].astype(F32)
            for m in range(1, g_ref.shape[0]):
                v = v + g_ref[m, at : at + 48, :].astype(F32)
            for k in range(4):
                o_ref[k % 2, pair * 2 + k // 2, zl, 0] = to_piece(v[k * ROWS : (k + 1) * ROWS])

    @pl.when(pl.program_id(0) == 0)
    def _():
        for j, r in enumerate((ma_ref, m1_ref, m2_ref)):
            st_ref[:, j] = jnp.broadcast_to(to_piece(r[...])[None], (ZH, PR, PC))


def micro_sum(local, *state):
    rows = ZL * X * C * ROWS
    return pl.pallas_call(
        sum_kernel,
        out_shape=(
            jax.ShapeDtypeStruct((C, X, ZL, ZH, PR, PC), F32),
            jax.ShapeDtypeStruct((ZH, 3, PR, PC), F32),
        ),
        grid=(ZH,),
        in_specs=[pl.BlockSpec((local.shape[0], rows, COLS), lambda i: (0, i, 0))]
        + [pl.BlockSpec((ROWS, COLS), lambda i: (0, 0))] * 3,
        out_specs=(
            pl.BlockSpec((C, X, ZL, 1, PR, PC), lambda i: (0, 0, 0, i, 0, 0)),
            pl.BlockSpec((ZH, 3, PR, PC), lambda i: (0, 0, 0, 0)),
        ),
        name="micro_sum",
    )(local, *state)


def adam(scale, total, master, moment1, moment2):
    clipped = scale * total
    m1 = BETA_ONE * moment1 + (1.0 - BETA_ONE) * clipped
    m2 = BETA_TWO * moment2 + (1.0 - BETA_TWO) * clipped * clipped
    first_hat = m1 / (1.0 - BETA_ONE**STEP)
    second_hat = m2 / (1.0 - BETA_TWO**STEP)
    new = master - LEARN_RATE * (
        first_hat / (jnp.sqrt(second_hat) + 1e-08) + DECAY_WEIGHT * master
    )
    return new, m1, m2


def update_kernel(elements, sq_ref, t_ref, st_ref, ma_ref, m1_ref, m2_ref, em_ref, oma, om1, om2, oem, ow):
    sq = jnp.sum(jnp.sum(sq_ref[...], axis=0))
    sq = jnp.full((1, PC), sq, F32)
    scale = jnp.minimum(1.0, 1.0 / jnp.sqrt(sq / elements + 1e-06))
    for zh in range(ZH):
        new, _, _ = adam(scale, t_ref[zh], st_ref[zh, 0], st_ref[zh, 1], st_ref[zh, 2])
        ow[:, zh] = jnp.broadcast_to(new.astype(BF16)[None], (ow.shape[0], PR, PC))
    total = from_piece(t_ref[lax.axis_index("zh")])
    wide = jnp.concatenate([scale, scale], axis=1)
    new, m1, m2 = adam(wide, total, ma_ref[...], m1_ref[...], m2_ref[...])
    oma[...] = new
    om1[...] = m1
    om2[...] = m2
    oem[...] = EMA_KEEP * em_ref[...] + (1.0 - EMA_KEEP) * new


def place_kernel(w_ref, o_ref):
    for zl in range(ZL):
        for pair in range(X // 2):
            parts = [
                from_piece(w_ref[k % 2, pair * 2 + k // 2, zl, 0].astype(F32)) for k in range(4)
            ]
            at = zl * X * C * ROWS + pair * 48
            o_ref[at : at + 48, :] = jnp.concatenate(parts, axis=0).astype(BF16)


def place(w):
    rows = ZL * X * C * ROWS
    return pl.pallas_call(
        place_kernel,
        out_shape=jax.ShapeDtypeStruct((ZH * rows, COLS), BF16),
        grid=(ZH,),
        in_specs=[pl.BlockSpec((C, X, ZL, 1, PR, PC), lambda i: (0, 0, 0, i, 0, 0))],
        out_specs=pl.BlockSpec((rows, COLS), lambda i: (i, 0)),
        name="place",
    )(w)


def exchange(v, axes):
    return lax.all_to_all(v, axes, split_axis=0, concat_axis=0, tiled=True)


def copies(v, n):
    return jnp.broadcast_to(v[None], (n,) + v.shape)


def shards(grads, master, moment1, moment2, ema):
    local = grads[0]
    elements = local.shape[1] * local.shape[2] * T

    part, held = micro_sum(local, master, moment1, moment2)
    held = exchange(held, "zh")
    part = jnp.sum(exchange(part, "c"), axis=0)
    part = jnp.sum(exchange(part, "x"), axis=0)
    part, held = lax.optimization_barrier((part, held))
    part = jnp.sum(exchange(part, "zl"), axis=0)
    total = jnp.sum(exchange(copies(part, ZH), "zh"), axis=0)
    sq = jnp.sum((total * total).reshape(-1, 8, PC), axis=0)
    sq = jnp.sum(exchange(copies(sq, X * C * T), ("x", "c", "t")), axis=0)
    sq = exchange(copies(sq, ZL), "zl")

    state = jax.ShapeDtypeStruct((ROWS, COLS), F32)
    new_master, new_moment1, new_moment2, new_ema, w = pl.pallas_call(
        lambda *refs: update_kernel(elements, *refs),
        out_shape=(state, state, state, state, jax.ShapeDtypeStruct((ZL, ZH, PR, PC), BF16)),
        name="update",
    )(sq, total, held, master, moment1, moment2, ema)

    w = exchange(w, "zl")
    w = exchange(copies(w, X), "x")
    w = lax.all_gather(w, "c", axis=0, tiled=False)
    weights = place(w)
    return (new_master, new_moment1, new_moment2, new_ema, weights)


def solution(mesh):
    fine = Mesh(mesh.devices.reshape(ZH, ZL, X, C, T), ("zh", "zl", "x", "c", "t"))
    rows = ("zh", "zl", "x", "c")
    return jax.shard_map(
        shards,
        mesh=fine,
        in_specs=(P(rows, None, None, "t"),) + (P(rows, "t"),) * 4,
        out_specs=(P(rows, "t"),) * 4 + (P(None, "t"),),
        check_vma=False,
    )
```

```python
import jax
import jax.numpy as jnp
from jax import lax
from jax.experimental import pallas as pl
from jax.experimental.pallas import tpu as pltpu
from jax.sharding import Mesh, PartitionSpec as P

STEP = 10
BETA_ONE = 0.9
BETA_TWO = 0.95
LEARN_RATE = 0.02
DECAY_WEIGHT = 0.1
EMA_KEEP = 0.99

ZH, ZL, X, C, T = 4, 4, 4, 2, 4
ROWS, COLS = 12, 256
PR, PC = 24, 128

F32 = jnp.float32
BF16 = jnp.bfloat16


def to_piece(v):
    return jnp.concatenate([v[0:8, :PC], v[0:8, PC:], v[8:12, :PC], v[8:12, PC:]], axis=0)


def from_piece(p):
    top = jnp.concatenate([p[0:8], p[8:16]], axis=1)
    low = jnp.concatenate([p[16:20], p[20:24]], axis=1)
    return jnp.concatenate([top, low], axis=0)


def sum_kernel(g_ref, o_ref):
    for zl in range(ZL):
        for pair in range(X // 2):
            at = zl * X * C * ROWS + pair * 48
            v = g_ref[0, at : at + 48, :].astype(F32)
            for m in range(1, g_ref.shape[0]):
                v = v + g_ref[m, at : at + 48, :].astype(F32)
            for k in range(4):
                o_ref[k % 2, pair * 2 + k // 2, zl, 0] = to_piece(v[k * ROWS : (k + 1) * ROWS])


def micro_sum(local):
    rows = ZL * X * C * ROWS
    return pl.pallas_call(
        sum_kernel,
        out_shape=jax.ShapeDtypeStruct((C, X, ZL, ZH, PR, PC), F32),
        grid=(ZH,),
        in_specs=[pl.BlockSpec((local.shape[0], rows, COLS), lambda i: (0, i, 0))],
        out_specs=pl.BlockSpec((C, X, ZL, 1, PR, PC), lambda i: (0, 0, 0, i, 0, 0)),
        name="micro_sum",
    )(local)


def adam(scale, total, master, moment1, moment2):
    clipped = scale * total
    m1 = BETA_ONE * moment1 + (1.0 - BETA_ONE) * clipped
    m2 = BETA_TWO * moment2 + (1.0 - BETA_TWO) * clipped * clipped
    first_hat = m1 / (1.0 - BETA_ONE**STEP)
    second_hat = m2 / (1.0 - BETA_TWO**STEP)
    new = master - LEARN_RATE * (
        first_hat / (jnp.sqrt(second_hat) + 1e-08) + DECAY_WEIGHT * master
    )
    return new, m1, m2


def update_kernel(elements, sq_ref, t_ref, ma_ref, m1_ref, m2_ref, em_ref, oma, om1, om2, oem, ow):
    sq = jnp.sum(jnp.sum(sq_ref[...], axis=0))
    sq = jnp.full((1, COLS), sq, F32)
    scale = jnp.minimum(1.0, 1.0 / jnp.sqrt(sq / elements + 1e-06))
    total = from_piece(t_ref[lax.axis_index("zh")])
    new, m1, m2 = adam(scale, total, ma_ref[...], m1_ref[...], m2_ref[...])
    oma[...] = new
    om1[...] = m1
    om2[...] = m2
    oem[...] = EMA_KEEP * em_ref[...] + (1.0 - EMA_KEEP) * new
    ow[...] = jnp.broadcast_to(to_piece(new).astype(BF16)[None, None], ow.shape)


def place_kernel(w_ref, o_ref):
    for zl in range(ZL):
        for pair in range(X // 2):
            parts = [
                from_piece(w_ref[k % 2, pair * 2 + k // 2, 0, zl].astype(F32)) for k in range(4)
            ]
            at = zl * X * C * ROWS + pair * 48
            o_ref[at : at + 48, :] = jnp.concatenate(parts, axis=0).astype(BF16)


def place(w):
    rows = ZL * X * C * ROWS
    return pl.pallas_call(
        place_kernel,
        out_shape=jax.ShapeDtypeStruct((ZH * rows, COLS), BF16),
        grid=(ZH,),
        in_specs=[pl.BlockSpec((C, X, 1, ZL, PR, PC), lambda i: (0, 0, i, 0, 0, 0))],
        out_specs=pl.BlockSpec((rows, COLS), lambda i: (i, 0)),
        name="place",
    )(w)


def exchange(v, axes):
    return lax.all_to_all(v, axes, split_axis=0, concat_axis=0, tiled=True)


def copies(v, n):
    return jnp.broadcast_to(v[None], (n,) + v.shape)


def shards(grads, master, moment1, moment2, ema):
    local = grads[0]
    elements = local.shape[1] * local.shape[2] * T

    part = micro_sum(local)
    part = jnp.sum(exchange(part, "c"), axis=0)
    part = jnp.sum(exchange(part, "x"), axis=0)
    part = jnp.sum(exchange(part, "zl"), axis=0)
    total = jnp.sum(exchange(copies(part, ZH), "zh"), axis=0)
    sq = jnp.sum((total * total).reshape(-1, 8, PC), axis=0)
    sq = jnp.sum(exchange(copies(sq, X * C * T), ("x", "c", "t")), axis=0)
    sq = exchange(copies(sq, ZL), "zl")

    state = jax.ShapeDtypeStruct((ROWS, COLS), F32)
    new_master, new_moment1, new_moment2, new_ema, w = pl.pallas_call(
        lambda *refs: update_kernel(elements, *refs),
        out_shape=(state, state, state, state, jax.ShapeDtypeStruct((ZH * ZL, 1, PR, PC), BF16)),
        name="update",
    )(sq, total, master, moment1, moment2, ema)

    w = exchange(w, ("zh", "zl")).reshape(ZH, ZL, PR, PC)
    w = exchange(copies(w, X), "x")
    w = lax.all_gather(w, "c", axis=0, tiled=False)
    weights = place(w)
    return (new_master, new_moment1, new_moment2, new_ema, weights)


def solution(mesh):
    fine = Mesh(mesh.devices.reshape(ZH, ZL, X, C, T), ("zh", "zl", "x", "c", "t"))
    rows = ("zh", "zl", "x", "c")
    return jax.shard_map(
        shards,
        mesh=fine,
        in_specs=(P(rows, None, None, "t"),) + (P(rows, "t"),) * 4,
        out_specs=(P(rows, "t"),) * 4 + (P(None, "t"),),
        check_vma=False,
    )
```

```python
import jax
import jax.numpy as jnp
from jax import lax
from jax.experimental import pallas as pl
from jax.experimental.pallas import tpu as pltpu
from jax.sharding import Mesh, PartitionSpec as P

STEP = 10
BETA_ONE = 0.9
BETA_TWO = 0.95
LEARN_RATE = 0.02
DECAY_WEIGHT = 0.1
EMA_KEEP = 0.99

ZH, ZL, X, C, T = 4, 4, 4, 2, 4
ROWS, COLS = 12, 256
PR, PC = 24, 128

F32 = jnp.float32
BF16 = jnp.bfloat16


def to_piece(v):
    return jnp.concatenate([v[0:8, :PC], v[0:8, PC:], v[8:12, :PC], v[8:12, PC:]], axis=0)


def from_piece(p):
    top = jnp.concatenate([p[0:8], p[8:16]], axis=1)
    low = jnp.concatenate([p[16:20], p[20:24]], axis=1)
    return jnp.concatenate([top, low], axis=0)


def sum_kernel(g_ref, ma_ref, m1_ref, m2_ref, o_ref, st_ref):
    for zl in range(ZL):
        for pair in range(X // 2):
            at = zl * X * C * ROWS + pair * 48
            v = g_ref[0, at : at + 48, :].astype(F32)
            for m in range(1, g_ref.shape[0]):
                v = v + g_ref[m, at : at + 48, :].astype(F32)
            for k in range(4):
                o_ref[k % 2, pair * 2 + k // 2, zl, 0] = to_piece(v[k * ROWS : (k + 1) * ROWS])

    mine = lax.axis_index("zh") == pl.program_id(0)
    for j, r in enumerate((ma_ref, m1_ref, m2_ref)):
        piece = jnp.where(mine, to_piece(r[...]), 0.0)
        st_ref[:, 0, j] = jnp.broadcast_to(piece[None], (ZH, PR, PC))


def micro_sum(local, *state):
    rows = ZL * X * C * ROWS
    return pl.pallas_call(
        sum_kernel,
        out_shape=(
            jax.ShapeDtypeStruct((C, X, ZL, ZH, PR, PC), F32),
            jax.ShapeDtypeStruct((ZH, ZH, 3, PR, PC), F32),
        ),
        grid=(ZH,),
        in_specs=[pl.BlockSpec((local.shape[0], rows, COLS), lambda i: (0, i, 0))]
        + [pl.BlockSpec((ROWS, COLS), lambda i: (0, 0))] * 3,
        out_specs=(
            pl.BlockSpec((C, X, ZL, 1, PR, PC), lambda i: (0, 0, 0, i, 0, 0)),
            pl.BlockSpec((ZH, 1, 3, PR, PC), lambda i: (0, i, 0, 0, 0)),
        ),
        name="micro_sum",
    )(local, *state)


def adam(scale, total, master, moment1, moment2):
    clipped = scale * total
    m1 = BETA_ONE * moment1 + (1.0 - BETA_ONE) * clipped
    m2 = BETA_TWO * moment2 + (1.0 - BETA_TWO) * clipped * clipped
    first_hat = m1 / (1.0 - BETA_ONE**STEP)
    second_hat = m2 / (1.0 - BETA_TWO**STEP)
    new = master - LEARN_RATE * (
        first_hat / (jnp.sqrt(second_hat) + 1e-08) + DECAY_WEIGHT * master
    )
    return new, m1, m2


def update_kernel(elements, sq_ref, t_ref, st_ref, ma_ref, m1_ref, m2_ref, em_ref, oma, om1, om2, oem, ow):
    sq = jnp.sum(jnp.sum(sq_ref[...], axis=0))
    sq = jnp.full((1, PC), sq, F32)
    scale = jnp.minimum(1.0, 1.0 / jnp.sqrt(sq / elements + 1e-06))
    for zh in range(ZH):
        new, _, _ = adam(scale, t_ref[zh], st_ref[zh, 0], st_ref[zh, 1], st_ref[zh, 2])
        ow[:, zh] = jnp.broadcast_to(new.astype(BF16)[None], (ow.shape[0], PR, PC))
    total = from_piece(t_ref[lax.axis_index("zh")])
    wide = jnp.concatenate([scale, scale], axis=1)
    new, m1, m2 = adam(wide, total, ma_ref[...], m1_ref[...], m2_ref[...])
    oma[...] = new
    om1[...] = m1
    om2[...] = m2
    oem[...] = EMA_KEEP * em_ref[...] + (1.0 - EMA_KEEP) * new


def place_kernel(w_ref, o_ref):
    for zl in range(ZL):
        for pair in range(X // 2):
            parts = [
                from_piece(w_ref[k % 2, pair * 2 + k // 2, zl, 0].astype(F32)) for k in range(4)
            ]
            at = zl * X * C * ROWS + pair * 48
            o_ref[at : at + 48, :] = jnp.concatenate(parts, axis=0).astype(BF16)


def place(w):
    rows = ZL * X * C * ROWS
    return pl.pallas_call(
        place_kernel,
        out_shape=jax.ShapeDtypeStruct((ZH * rows, COLS), BF16),
        grid=(ZH,),
        in_specs=[pl.BlockSpec((C, X, ZL, 1, PR, PC), lambda i: (0, 0, 0, i, 0, 0))],
        out_specs=pl.BlockSpec((rows, COLS), lambda i: (i, 0)),
        name="place",
    )(w)


def exchange(v, axes):
    return lax.all_to_all(v, axes, split_axis=0, concat_axis=0, tiled=True)


def copies(v, n):
    return jnp.broadcast_to(v[None], (n,) + v.shape)


def shards(grads, master, moment1, moment2, ema):
    local = grads[0]
    elements = local.shape[1] * local.shape[2] * T

    part, slots = micro_sum(local, master, moment1, moment2)
    held = lax.psum_scatter(slots, "zh", scatter_dimension=0, tiled=False)
    part = jnp.sum(exchange(part, "c"), axis=0)
    part = jnp.sum(exchange(part, "x"), axis=0)
    part = jnp.sum(exchange(part, "zl"), axis=0)
    total = jnp.sum(exchange(copies(part, ZH), "zh"), axis=0)
    sq = jnp.sum((total * total).reshape(-1, 8, PC), axis=0)
    sq = jnp.sum(exchange(copies(sq, X * C * T), ("x", "c", "t")), axis=0)
    sq = exchange(copies(sq, ZL), "zl")

    state = jax.ShapeDtypeStruct((ROWS, COLS), F32)
    new_master, new_moment1, new_moment2, new_ema, w = pl.pallas_call(
        lambda *refs: update_kernel(elements, *refs),
        out_shape=(state, state, state, state, jax.ShapeDtypeStruct((ZL, ZH, PR, PC), BF16)),
        name="update",
    )(sq, total, held, master, moment1, moment2, ema)

    w = exchange(w, "zl")
    w = exchange(copies(w, X), "x")
    w = lax.all_gather(w, "c", axis=0, tiled=False)
    weights = place(w)
    return (new_master, new_moment1, new_moment2, new_ema, weights)


def solution(mesh):
    fine = Mesh(mesh.devices.reshape(ZH, ZL, X, C, T), ("zh", "zl", "x", "c", "t"))
    rows = ("zh", "zl", "x", "c")
    return jax.shard_map(
        shards,
        mesh=fine,
        in_specs=(P(rows, None, None, "t"),) + (P(rows, "t"),) * 4,
        out_specs=(P(rows, "t"),) * 4 + (P(None, "t"),),
        check_vma=False,
    )
```

```python
import jax
import jax.numpy as jnp
from jax import lax
from jax.experimental import pallas as pl
from jax.experimental.pallas import tpu as pltpu
from jax.sharding import Mesh, PartitionSpec as P

STEP = 10
BETA_ONE = 0.9
BETA_TWO = 0.95
LEARN_RATE = 0.02
DECAY_WEIGHT = 0.1
EMA_KEEP = 0.99

ZH, ZL, X, C, T = 4, 4, 4, 2, 4
ROWS, COLS = 12, 256
PR, PC = 24, 128
GROUP = C * ROWS
STEPS = 2
NZH = ZH // STEPS

F32 = jnp.float32
BF16 = jnp.bfloat16


def upper():
    return lax.broadcasted_iota(jnp.int32, (8, PC), 0) < 4


def shared_tile(core, left, right):
    turned = pltpu.roll(right, 4, 0)
    return jnp.where(upper(), left, turned) if core == 0 else jnp.where(upper(), turned, left)


def to_piece(core, v):
    zero = [v[0:8, :PC], v[0:8, PC:], v[8:12, :PC], v[8:12, PC:]]
    one = [v[4:12, :PC], v[4:12, PC:], v[0:4, PC:], v[0:4, :PC]]
    return jnp.where(core == 0, jnp.concatenate(zero, axis=0), jnp.concatenate(one, axis=0))


def from_piece(core, p):
    full = jnp.concatenate([p[0:8], p[8:16]], axis=1)
    zero = jnp.concatenate([full, jnp.concatenate([p[16:20], p[20:24]], axis=1)], axis=0)
    one = jnp.concatenate([jnp.concatenate([p[20:24], p[16:20]], axis=1), full], axis=0)
    return jnp.where(core == 0, zero, one)


def half_body(core, g_ref, o_ref):
    me = lax.axis_index("x")
    for zh in range(NZH):
        for zl in range(ZL):
            for x in range(X):
                at = ((zh * ZL + zl) * X + x) * GROUP + 8 * core
                v = g_ref[0, at : at + 16, :].astype(F32)
                for m in range(1, g_ref.shape[0]):
                    v = v + g_ref[m, at : at + 16, :].astype(F32)
                own, both = (v[0:8], v[8:16]) if core == 0 else (v[8:16], v[0:8])
                o = o_ref.at[lax.rem(x + X - me, X), zl, zh]
                o[0:8] = own[:, :PC]
                o[8:16] = own[:, PC:]
                o[16:24] = shared_tile(core, both[:, :PC], both[:, PC:])


def half_pieces(core, g_ref, o_ref):
    for k in range(C):
        pl.when(core == k)(lambda k=k: half_body(k, g_ref, o_ref))


def other_kernel(g_ref, ma_ref, m1_ref, m2_ref, o_ref, st_ref):
    core = lax.axis_index("c")
    half_pieces(1 - core, g_ref, o_ref)

    @pl.when(pl.program_id(0) == 0)
    def _():
        for j, r in enumerate((ma_ref, m1_ref, m2_ref)):
            st_ref[:, j] = jnp.broadcast_to(to_piece(core, r[...])[None], (ZH, PR, PC))


def own_kernel(g_ref, o_ref):
    half_pieces(lax.axis_index("c"), g_ref, o_ref)


def half_specs(local):
    rows = NZH * ZL * X * GROUP
    shape = jax.ShapeDtypeStruct((X, ZL, ZH, PR, PC), F32)
    source = pl.BlockSpec((local.shape[0], rows, COLS), lambda i: (0, i, 0))
    target = pl.BlockSpec((X, ZL, NZH, PR, PC), lambda i: (0, 0, i, 0, 0))
    cost = pl.CostEstimate(flops=2_000_000, bytes_accessed=4_000_000, transcendentals=0)
    return shape, source, target, cost


def other_sum(local, *state):
    shape, source, target, cost = half_specs(local)
    return pl.pallas_call(
        other_kernel,
        out_shape=(shape, jax.ShapeDtypeStruct((ZH, 3, PR, PC), F32)),
        grid=(STEPS,),
        in_specs=[source] + [pl.BlockSpec((ROWS, COLS), lambda i: (0, 0))] * 3,
        out_specs=(target, pl.BlockSpec((ZH, 3, PR, PC), lambda i: (0, 0, 0, 0))),
        cost_estimate=cost,
        name="other_sum",
    )(local, *state)


def own_sum(local):
    shape, source, target, cost = half_specs(local)
    return pl.pallas_call(
        own_kernel,
        out_shape=shape,
        grid=(STEPS,),
        in_specs=[source],
        out_specs=target,
        cost_estimate=cost,
        name="own_sum",
    )(local)


def adam(scale, total, master, moment1, moment2):
    clipped = scale * total
    m1 = BETA_ONE * moment1 + (1.0 - BETA_ONE) * clipped
    m2 = BETA_TWO * moment2 + (1.0 - BETA_TWO) * clipped * clipped
    first_hat = m1 / (1.0 - BETA_ONE**STEP)
    second_hat = m2 / (1.0 - BETA_TWO**STEP)
    new = master - LEARN_RATE * (
        first_hat / (jnp.sqrt(second_hat) + 1e-08) + DECAY_WEIGHT * master
    )
    return new, m1, m2


def update_kernel(elements, sq_ref, t_ref, st_ref, ma_ref, m1_ref, m2_ref, em_ref, oma, om1, om2, oem, ow):
    sq = jnp.sum(jnp.sum(sq_ref[...], axis=0))
    sq = jnp.full((1, PC), sq, F32)
    scale = jnp.minimum(1.0, 1.0 / jnp.sqrt(sq / elements + 1e-06))
    for zh in range(ZH):
        new, _, _ = adam(scale, t_ref[zh], st_ref[zh, 0], st_ref[zh, 1], st_ref[zh, 2])
        ow[:, zh] = jnp.broadcast_to(new.astype(BF16)[None], (ow.shape[0], PR, PC))
    total = from_piece(lax.axis_index("c"), t_ref[lax.axis_index("zh")])
    wide = jnp.concatenate([scale, scale], axis=1)
    new, m1, m2 = adam(wide, total, ma_ref[...], m1_ref[...], m2_ref[...])
    oma[...] = new
    om1[...] = m1
    om2[...] = m2
    oem[...] = EMA_KEEP * em_ref[...] + (1.0 - EMA_KEEP) * new


def place_kernel(w_ref, o_ref):
    for zh in range(NZH):
        for zl in range(ZL):
            for x in range(X):
                at = ((zh * ZL + zl) * X + x) * GROUP
                a, b = w_ref.at[0, x, zl, zh], w_ref.at[1, x, zl, zh]
                o_ref[at : at + 8, :PC] = a[0:8]
                o_ref[at : at + 8, PC:] = a[8:16]
                o_ref[at + 16 : at + 24, :PC] = b[0:8]
                o_ref[at + 16 : at + 24, PC:] = b[8:16]
                p, q = a[16:24].astype(F32), b[16:24].astype(F32)
                left = jnp.where(upper(), p, q)
                right = pltpu.roll(jnp.where(upper(), q, p), 4, 0)
                o_ref[at + 8 : at + 16, :PC] = left.astype(BF16)
                o_ref[at + 8 : at + 16, PC:] = right.astype(BF16)


def place(w):
    rows = NZH * ZL * X * GROUP
    return pl.pallas_call(
        place_kernel,
        out_shape=jax.ShapeDtypeStruct((STEPS * rows, COLS), BF16),
        grid=(STEPS,),
        in_specs=[pl.BlockSpec((C, X, ZL, NZH, PR, PC), lambda i: (0, 0, 0, i, 0, 0))],
        out_specs=pl.BlockSpec((rows, COLS), lambda i: (i, 0)),
        name="place",
    )(w)


def exchange(v, axes):
    return lax.all_to_all(v, axes, split_axis=0, concat_axis=0, tiled=True)


def copies(v, n):
    return jnp.broadcast_to(v[None], (n,) + v.shape)


def shift(v, axis, n, k):
    return lax.ppermute(v, axis, [(i, (i + k) % n) for i in range(n)])


def shards(grads, master, moment1, moment2, ema):
    local = grads[0]
    elements = local.shape[1] * local.shape[2] * T

    other, held = other_sum(local, master, moment1, moment2)
    held = exchange(held, "zh")
    part = own_sum(local) + shift(other, "c", C, 1)
    part = part[0] + sum(shift(part[k], "x", X, k) for k in range(1, X))
    part, held = lax.optimization_barrier((part, held))
    part = jnp.sum(exchange(part, "zl"), axis=0)
    total = jnp.sum(exchange(copies(part, ZH), "zh"), axis=0)
    sq = jnp.sum((total * total).reshape(-1, 8, PC), axis=0)
    sq = jnp.sum(exchange(copies(sq, X * C * T), ("x", "c", "t")), axis=0)
    sq = exchange(copies(sq, ZL), "zl")

    state = jax.ShapeDtypeStruct((ROWS, COLS), F32)
    new_master, new_moment1, new_moment2, new_ema, w = pl.pallas_call(
        lambda *refs: update_kernel(elements, *refs),
        out_shape=(state, state, state, state, jax.ShapeDtypeStruct((ZL, ZH, PR, PC), BF16)),
        name="update",
    )(sq, total, held, master, moment1, moment2, ema)

    w = exchange(w, "zl")
    w = exchange(copies(w, X), "x")
    w = lax.all_gather(w, "c", axis=0, tiled=False)
    weights = place(w)
    return (new_master, new_moment1, new_moment2, new_ema, weights)


def solution(mesh):
    fine = Mesh(mesh.devices.reshape(ZH, ZL, X, C, T), ("zh", "zl", "x", "c", "t"))
    rows = ("zh", "zl", "x", "c")
    return jax.shard_map(
        shards,
        mesh=fine,
        in_specs=(P(rows, None, None, "t"),) + (P(rows, "t"),) * 4,
        out_specs=(P(rows, "t"),) * 4 + (P(None, "t"),),
        check_vma=False,
    )
```

```python
import jax
import jax.numpy as jnp
from jax import lax
from jax.experimental import pallas as pl
from jax.experimental.pallas import tpu as pltpu
from jax.sharding import Mesh, PartitionSpec as P

STEP = 10
BETA_ONE = 0.9
BETA_TWO = 0.95
LEARN_RATE = 0.02
DECAY_WEIGHT = 0.1
EMA_KEEP = 0.99

ZH, ZL, X, C, T = 4, 4, 4, 2, 4
ROWS, COLS = 12, 256
PR, PC = 24, 128
GROUP = C * ROWS
STEPS = 2
NZH = ZH // STEPS

F32 = jnp.float32
BF16 = jnp.bfloat16


def upper():
    return lax.broadcasted_iota(jnp.int32, (8, PC), 0) < 4


def shared_tile(core, left, right):
    turned = pltpu.roll(right, 4, 0)
    return jnp.where(upper(), left, turned) if core == 0 else jnp.where(upper(), turned, left)


def to_piece(core, v):
    zero = [v[0:8, :PC], v[0:8, PC:], v[8:12, :PC], v[8:12, PC:]]
    one = [v[4:12, :PC], v[4:12, PC:], v[0:4, PC:], v[0:4, :PC]]
    return jnp.where(core == 0, jnp.concatenate(zero, axis=0), jnp.concatenate(one, axis=0))


def from_piece(core, p):
    full = jnp.concatenate([p[0:8], p[8:16]], axis=1)
    zero = jnp.concatenate([full, jnp.concatenate([p[16:20], p[20:24]], axis=1)], axis=0)
    one = jnp.concatenate([jnp.concatenate([p[20:24], p[16:20]], axis=1), full], axis=0)
    return jnp.where(core == 0, zero, one)


def half_body(core, g_ref, o_ref):
    me = lax.axis_index("x")
    for zh in range(NZH):
        for zl in range(ZL):
            for x in range(X):
                at = ((zh * ZL + zl) * X + x) * GROUP + 8 * core
                v = g_ref[0, at : at + 16, :].astype(F32)
                for m in range(1, g_ref.shape[0]):
                    v = v + g_ref[m, at : at + 16, :].astype(F32)
                own, both = (v[0:8], v[8:16]) if core == 0 else (v[8:16], v[0:8])
                o = o_ref.at[lax.rem(x + X - me, X), zl, zh]
                o[0:8] = own[:, :PC]
                o[8:16] = own[:, PC:]
                o[16:24] = shared_tile(core, both[:, :PC], both[:, PC:])


def half_pieces(core, g_ref, o_ref):
    for k in range(C):
        pl.when(core == k)(lambda k=k: half_body(k, g_ref, o_ref))


def other_kernel(g_ref, ma_ref, m1_ref, m2_ref, o_ref, st_ref):
    core = lax.axis_index("c")
    half_pieces(1 - core, g_ref, o_ref)

    @pl.when(pl.program_id(0) == 0)
    def _():
        for j, r in enumerate((ma_ref, m1_ref, m2_ref)):
            st_ref[j] = to_piece(core, r[...])


def own_kernel(g_ref, o_ref):
    half_pieces(lax.axis_index("c"), g_ref, o_ref)


def half_specs(local):
    rows = NZH * ZL * X * GROUP
    shape = jax.ShapeDtypeStruct((X, ZL, ZH, PR, PC), F32)
    source = pl.BlockSpec((local.shape[0], rows, COLS), lambda i: (0, i, 0))
    target = pl.BlockSpec((X, ZL, NZH, PR, PC), lambda i: (0, 0, i, 0, 0))
    cost = pl.CostEstimate(flops=2_000_000, bytes_accessed=4_000_000, transcendentals=0)
    return shape, source, target, cost


def other_sum(local, *state):
    shape, source, target, cost = half_specs(local)
    return pl.pallas_call(
        other_kernel,
        out_shape=(shape, jax.ShapeDtypeStruct((3, PR, PC), F32)),
        grid=(STEPS,),
        in_specs=[source] + [pl.BlockSpec((ROWS, COLS), lambda i: (0, 0))] * 3,
        out_specs=(target, pl.BlockSpec((3, PR, PC), lambda i: (0, 0, 0))),
        cost_estimate=cost,
        name="other_sum",
    )(local, *state)


def own_sum(local):
    shape, source, target, cost = half_specs(local)
    return pl.pallas_call(
        own_kernel,
        out_shape=shape,
        grid=(STEPS,),
        in_specs=[source],
        out_specs=target,
        cost_estimate=cost,
        name="own_sum",
    )(local)


def adam(scale, total, master, moment1, moment2):
    clipped = scale * total
    m1 = BETA_ONE * moment1 + (1.0 - BETA_ONE) * clipped
    m2 = BETA_TWO * moment2 + (1.0 - BETA_TWO) * clipped * clipped
    first_hat = m1 / (1.0 - BETA_ONE**STEP)
    second_hat = m2 / (1.0 - BETA_TWO**STEP)
    new = master - LEARN_RATE * (
        first_hat / (jnp.sqrt(second_hat) + 1e-08) + DECAY_WEIGHT * master
    )
    return new, m1, m2


def update_kernel(elements, sq_ref, t_ref, s0, s1, s2, s3, ma_ref, m1_ref, m2_ref, em_ref, oma, om1, om2, oem, ow):
    sq = jnp.sum(jnp.sum(sq_ref[...], axis=0))
    sq = jnp.full((1, PC), sq, F32)
    scale = jnp.minimum(1.0, 1.0 / jnp.sqrt(sq / elements + 1e-06))
    me = lax.axis_index("zh")
    for k, st in enumerate((s0, s1, s2, s3)):
        zh = lax.rem(me + ZH - k, ZH)
        new, _, _ = adam(scale, t_ref[zh], st[0], st[1], st[2])
        ow[:, zh] = jnp.broadcast_to(new.astype(BF16)[None], (ow.shape[0], PR, PC))
    total = from_piece(lax.axis_index("c"), t_ref[me])
    wide = jnp.concatenate([scale, scale], axis=1)
    new, m1, m2 = adam(wide, total, ma_ref[...], m1_ref[...], m2_ref[...])
    oma[...] = new
    om1[...] = m1
    om2[...] = m2
    oem[...] = EMA_KEEP * em_ref[...] + (1.0 - EMA_KEEP) * new


def place_kernel(w_ref, o_ref):
    for zh in range(NZH):
        for zl in range(ZL):
            for x in range(X):
                at = ((zh * ZL + zl) * X + x) * GROUP
                a, b = w_ref.at[0, x, zl, zh], w_ref.at[1, x, zl, zh]
                o_ref[at : at + 8, :PC] = a[0:8]
                o_ref[at : at + 8, PC:] = a[8:16]
                o_ref[at + 16 : at + 24, :PC] = b[0:8]
                o_ref[at + 16 : at + 24, PC:] = b[8:16]
                p, q = a[16:24].astype(F32), b[16:24].astype(F32)
                left = jnp.where(upper(), p, q)
                right = pltpu.roll(jnp.where(upper(), q, p), 4, 0)
                o_ref[at + 8 : at + 16, :PC] = left.astype(BF16)
                o_ref[at + 8 : at + 16, PC:] = right.astype(BF16)


def place(w):
    rows = NZH * ZL * X * GROUP
    return pl.pallas_call(
        place_kernel,
        out_shape=jax.ShapeDtypeStruct((STEPS * rows, COLS), BF16),
        grid=(STEPS,),
        in_specs=[pl.BlockSpec((C, X, ZL, NZH, PR, PC), lambda i: (0, 0, 0, i, 0, 0))],
        out_specs=pl.BlockSpec((rows, COLS), lambda i: (i, 0)),
        name="place",
    )(w)


def exchange(v, axes):
    return lax.all_to_all(v, axes, split_axis=0, concat_axis=0, tiled=True)


def copies(v, n):
    return jnp.broadcast_to(v[None], (n,) + v.shape)


def shift(v, axis, n, k):
    return lax.ppermute(v, axis, [(i, (i + k) % n) for i in range(n)])


def shards(grads, master, moment1, moment2, ema):
    local = grads[0]
    elements = local.shape[1] * local.shape[2] * T

    other, held = other_sum(local, master, moment1, moment2)
    held = [held] + [shift(held, "zh", ZH, k) for k in range(1, ZH)]
    part = own_sum(local) + shift(other, "c", C, 1)
    part = part[0] + sum(shift(part[k], "x", X, k) for k in range(1, X))
    part, held = lax.optimization_barrier((part, held))
    part = jnp.sum(exchange(part, "zl"), axis=0)
    total = jnp.sum(exchange(copies(part, ZH), "zh"), axis=0)
    sq = jnp.sum((total * total).reshape(-1, 8, PC), axis=0)
    sq = jnp.sum(exchange(copies(sq, X * C * T), ("x", "c", "t")), axis=0)
    sq = exchange(copies(sq, ZL), "zl")

    state = jax.ShapeDtypeStruct((ROWS, COLS), F32)
    new_master, new_moment1, new_moment2, new_ema, w = pl.pallas_call(
        lambda *refs: update_kernel(elements, *refs),
        out_shape=(state, state, state, state, jax.ShapeDtypeStruct((ZL, ZH, PR, PC), BF16)),
        name="update",
    )(sq, total, *held, master, moment1, moment2, ema)

    w = exchange(w, "zl")
    w = exchange(copies(w, X), "x")
    w = lax.all_gather(w, "c", axis=0, tiled=False)
    weights = place(w)
    return (new_master, new_moment1, new_moment2, new_ema, weights)


def solution(mesh):
    fine = Mesh(mesh.devices.reshape(ZH, ZL, X, C, T), ("zh", "zl", "x", "c", "t"))
    rows = ("zh", "zl", "x", "c")
    return jax.shard_map(
        shards,
        mesh=fine,
        in_specs=(P(rows, None, None, "t"),) + (P(rows, "t"),) * 4,
        out_specs=(P(rows, "t"),) * 4 + (P(None, "t"),),
        check_vma=False,
    )
```

```python
import jax
import jax.numpy as jnp
from jax import lax
from jax.experimental import pallas as pl
from jax.experimental.pallas import tpu as pltpu
from jax.sharding import Mesh, PartitionSpec as P

STEP = 10
BETA_ONE = 0.9
BETA_TWO = 0.95
LEARN_RATE = 0.02
DECAY_WEIGHT = 0.1
EMA_KEEP = 0.99

ZH, ZL, X, C, T = 4, 4, 4, 2, 4
ROWS, COLS = 12, 256
PR, PC = 24, 128
GROUP = C * ROWS
STEPS = 2
NZH = ZH // STEPS

F32 = jnp.float32
BF16 = jnp.bfloat16


def upper():
    return lax.broadcasted_iota(jnp.int32, (8, PC), 0) < 4


def shared_tile(core, left, right):
    turned = pltpu.roll(right, 4, 0)
    return jnp.where(upper(), left, turned) if core == 0 else jnp.where(upper(), turned, left)


def to_piece(core, v):
    zero = [v[0:8, :PC], v[0:8, PC:], v[8:12, :PC], v[8:12, PC:]]
    one = [v[4:12, :PC], v[4:12, PC:], v[0:4, PC:], v[0:4, :PC]]
    return jnp.where(core == 0, jnp.concatenate(zero, axis=0), jnp.concatenate(one, axis=0))


def from_piece(core, p):
    full = jnp.concatenate([p[0:8], p[8:16]], axis=1)
    zero = jnp.concatenate([full, jnp.concatenate([p[16:20], p[20:24]], axis=1)], axis=0)
    one = jnp.concatenate([jnp.concatenate([p[20:24], p[16:20]], axis=1), full], axis=0)
    return jnp.where(core == 0, zero, one)


def half_body(core, g_ref, o_ref):
    me = lax.axis_index("x")
    for zh in range(NZH):
        for zl in range(ZL):
            for x in range(X):
                at = ((zh * ZL + zl) * X + x) * GROUP + 8 * core
                v = g_ref[0, at : at + 16, :].astype(F32)
                for m in range(1, g_ref.shape[0]):
                    v = v + g_ref[m, at : at + 16, :].astype(F32)
                own, both = (v[0:8], v[8:16]) if core == 0 else (v[8:16], v[0:8])
                o = o_ref.at[lax.rem(x + X - me, X), zl, zh]
                o[0:8] = own[:, :PC]
                o[8:16] = own[:, PC:]
                o[16:24] = shared_tile(core, both[:, :PC], both[:, PC:])


def half_pieces(core, g_ref, o_ref):
    for k in range(C):
        pl.when(core == k)(lambda k=k: half_body(k, g_ref, o_ref))


def other_kernel(g_ref, ma_ref, m1_ref, m2_ref, o_ref, st_ref):
    core = lax.axis_index("c")
    half_pieces(1 - core, g_ref, o_ref)

    @pl.when(pl.program_id(0) == 0)
    def _():
        for j, r in enumerate((ma_ref, m1_ref, m2_ref)):
            st_ref[:, j] = jnp.broadcast_to(to_piece(core, r[...])[None], (ZH, PR, PC))


def own_kernel(g_ref, o_ref):
    half_pieces(lax.axis_index("c"), g_ref, o_ref)


def half_specs(local):
    rows = NZH * ZL * X * GROUP
    shape = jax.ShapeDtypeStruct((X, ZL, ZH, PR, PC), F32)
    source = pl.BlockSpec((local.shape[0], rows, COLS), lambda i: (0, i, 0))
    target = pl.BlockSpec((X, ZL, NZH, PR, PC), lambda i: (0, 0, i, 0, 0))
    cost = pl.CostEstimate(flops=2_000_000, bytes_accessed=4_000_000, transcendentals=0)
    return shape, source, target, cost


def other_sum(local, *state):
    shape, source, target, cost = half_specs(local)
    return pl.pallas_call(
        other_kernel,
        out_shape=(shape, jax.ShapeDtypeStruct((ZH, 3, PR, PC), F32)),
        grid=(STEPS,),
        in_specs=[source] + [pl.BlockSpec((ROWS, COLS), lambda i: (0, 0))] * 3,
        out_specs=(target, pl.BlockSpec((ZH, 3, PR, PC), lambda i: (0, 0, 0, 0))),
        cost_estimate=cost,
        name="other_sum",
    )(local, *state)


def own_sum(local):
    shape, source, target, cost = half_specs(local)
    return pl.pallas_call(
        own_kernel,
        out_shape=shape,
        grid=(STEPS,),
        in_specs=[source],
        out_specs=target,
        cost_estimate=cost,
        name="own_sum",
    )(local)


def adam(scale, total, master, moment1, moment2):
    clipped = scale * total
    m1 = BETA_ONE * moment1 + (1.0 - BETA_ONE) * clipped
    m2 = BETA_TWO * moment2 + (1.0 - BETA_TWO) * clipped * clipped
    first_hat = m1 / (1.0 - BETA_ONE**STEP)
    second_hat = m2 / (1.0 - BETA_TWO**STEP)
    new = master - LEARN_RATE * (
        first_hat / (jnp.sqrt(second_hat) + 1e-08) + DECAY_WEIGHT * master
    )
    return new, m1, m2


def update_kernel(elements, sq_ref, t_ref, st_ref, ma_ref, m1_ref, m2_ref, em_ref, oma, om1, om2, oem, ow):
    sq = jnp.sum(jnp.sum(sq_ref[...], axis=0))
    sq = jnp.full((1, PC), sq, F32)
    scale = jnp.minimum(1.0, 1.0 / jnp.sqrt(sq / elements + 1e-06))
    for zh in range(ZH):
        new, _, _ = adam(scale, t_ref[zh], st_ref[zh, 0], st_ref[zh, 1], st_ref[zh, 2])
        ow[:, zh] = jnp.broadcast_to(new.astype(BF16)[None], (ow.shape[0], PR, PC))
    total = from_piece(lax.axis_index("c"), t_ref[lax.axis_index("zh")])
    wide = jnp.concatenate([scale, scale], axis=1)
    new, m1, m2 = adam(wide, total, ma_ref[...], m1_ref[...], m2_ref[...])
    oma[...] = new
    om1[...] = m1
    om2[...] = m2
    oem[...] = EMA_KEEP * em_ref[...] + (1.0 - EMA_KEEP) * new


def place_kernel(w_ref, o_ref):
    for zh in range(NZH):
        for zl in range(ZL):
            for x in range(X):
                at = ((zh * ZL + zl) * X + x) * GROUP
                a, b = w_ref.at[0, x, zl, zh], w_ref.at[1, x, zl, zh]
                o_ref[at : at + 8, :PC] = a[0:8]
                o_ref[at : at + 8, PC:] = a[8:16]
                o_ref[at + 16 : at + 24, :PC] = b[0:8]
                o_ref[at + 16 : at + 24, PC:] = b[8:16]
                p, q = a[16:24].astype(F32), b[16:24].astype(F32)
                left = jnp.where(upper(), p, q)
                right = pltpu.roll(jnp.where(upper(), q, p), 4, 0)
                o_ref[at + 8 : at + 16, :PC] = left.astype(BF16)
                o_ref[at + 8 : at + 16, PC:] = right.astype(BF16)


def place(w):
    rows = NZH * ZL * X * GROUP
    return pl.pallas_call(
        place_kernel,
        out_shape=jax.ShapeDtypeStruct((STEPS * rows, COLS), BF16),
        grid=(STEPS,),
        in_specs=[pl.BlockSpec((C, X, ZL, NZH, PR, PC), lambda i: (0, 0, 0, i, 0, 0))],
        out_specs=pl.BlockSpec((rows, COLS), lambda i: (i, 0)),
        name="place",
    )(w)


def exchange(v, axes):
    return lax.all_to_all(v, axes, split_axis=0, concat_axis=0, tiled=True)


def copies(v, n):
    return jnp.broadcast_to(v[None], (n,) + v.shape)


def shift(v, axis, n, k):
    return lax.ppermute(v, axis, [(i, (i + k) % n) for i in range(n)])


def shards(grads, master, moment1, moment2, ema):
    local = grads[0]
    elements = local.shape[1] * local.shape[2] * T

    other, held = other_sum(local, master, moment1, moment2)
    held = exchange(held, "zh")
    part = own_sum(local) + shift(other, "c", C, 1)
    parts = [part[0]] + [shift(part[k], "x", X, k) for k in range(1, X)]
    parts, held = lax.optimization_barrier((parts, held))
    part = parts[0] + parts[1] + parts[2] + parts[3]
    part = jnp.sum(exchange(part, "zl"), axis=0)
    total = jnp.sum(exchange(copies(part, ZH), "zh"), axis=0)
    sq = jnp.sum((total * total).reshape(-1, 8, PC), axis=0)
    sq = jnp.sum(exchange(copies(sq, X * C * T), ("x", "c", "t")), axis=0)
    sq = exchange(copies(sq, ZL), "zl")

    state = jax.ShapeDtypeStruct((ROWS, COLS), F32)
    new_master, new_moment1, new_moment2, new_ema, w = pl.pallas_call(
        lambda *refs: update_kernel(elements, *refs),
        out_shape=(state, state, state, state, jax.ShapeDtypeStruct((ZL, ZH, PR, PC), BF16)),
        name="update",
    )(sq, total, held, master, moment1, moment2, ema)

    w = exchange(w, "zl")
    w = exchange(copies(w, X), "x")
    w = lax.all_gather(w, "c", axis=0, tiled=False)
    weights = place(w)
    return (new_master, new_moment1, new_moment2, new_ema, weights)


def solution(mesh):
    fine = Mesh(mesh.devices.reshape(ZH, ZL, X, C, T), ("zh", "zl", "x", "c", "t"))
    rows = ("zh", "zl", "x", "c")
    return jax.shard_map(
        shards,
        mesh=fine,
        in_specs=(P(rows, None, None, "t"),) + (P(rows, "t"),) * 4,
        out_specs=(P(rows, "t"),) * 4 + (P(None, "t"),),
        check_vma=False,
    )
```

```python
import jax
import jax.numpy as jnp
from jax import lax
from jax.experimental import pallas as pl
from jax.experimental.pallas import tpu as pltpu
from jax.sharding import Mesh, PartitionSpec as P

STEP = 10
BETA_ONE = 0.9
BETA_TWO = 0.95
LEARN_RATE = 0.02
DECAY_WEIGHT = 0.1
EMA_KEEP = 0.99

Z, X, C, T = 16, 4, 2, 4
ROWS, COLS = 12, 256
PR, PC = 24, 128
GROUP = C * ROWS
STEPS = 2
NZ = Z // STEPS

F32 = jnp.float32
BF16 = jnp.bfloat16


def upper():
    return lax.broadcasted_iota(jnp.int32, (8, PC), 0) < 4


def shared_tile(core, left, right):
    turned = pltpu.roll(right, 4, 0)
    return jnp.where(upper(), left, turned) if core == 0 else jnp.where(upper(), turned, left)


def to_piece(core, v):
    zero = [v[0:8, :PC], v[0:8, PC:], v[8:12, :PC], v[8:12, PC:]]
    one = [v[4:12, :PC], v[4:12, PC:], v[0:4, PC:], v[0:4, :PC]]
    return jnp.where(core == 0, jnp.concatenate(zero, axis=0), jnp.concatenate(one, axis=0))


def from_piece(core, p):
    full = jnp.concatenate([p[0:8], p[8:16]], axis=1)
    zero = jnp.concatenate([full, jnp.concatenate([p[16:20], p[20:24]], axis=1)], axis=0)
    one = jnp.concatenate([jnp.concatenate([p[20:24], p[16:20]], axis=1), full], axis=0)
    return jnp.where(core == 0, zero, one)


def sum_kernel(g_ref, o_ref):
    for z in range(NZ):
        for pair in range(X // 2):
            at = (z * X + 2 * pair) * GROUP
            v = g_ref[0, at : at + 2 * GROUP, :].astype(F32)
            for m in range(1, g_ref.shape[0]):
                v = v + g_ref[m, at : at + 2 * GROUP, :].astype(F32)
            for k in range(2):
                first, both, last = [v[k * GROUP + j : k * GROUP + j + 8] for j in (0, 8, 16)]
                for core, own in ((0, first), (1, last)):
                    o = o_ref.at[core, 2 * pair + k, z]
                    o[0:8] = own[:, :PC]
                    o[8:16] = own[:, PC:]
                    o[16:24] = shared_tile(core, both[:, :PC], both[:, PC:])


def micro_sum(local):
    rows = NZ * X * GROUP
    return pl.pallas_call(
        sum_kernel,
        out_shape=jax.ShapeDtypeStruct((C, X, Z, PR, PC), F32),
        grid=(STEPS,),
        in_specs=[pl.BlockSpec((local.shape[0], rows, COLS), lambda i: (0, i, 0))],
        out_specs=pl.BlockSpec((C, X, NZ, PR, PC), lambda i: (0, 0, i, 0, 0)),
        name="micro_sum",
    )(local)


def adam(scale, total, master, moment1, moment2):
    clipped = scale * total
    m1 = BETA_ONE * moment1 + (1.0 - BETA_ONE) * clipped
    m2 = BETA_TWO * moment2 + (1.0 - BETA_TWO) * clipped * clipped
    first_hat = m1 / (1.0 - BETA_ONE**STEP)
    second_hat = m2 / (1.0 - BETA_TWO**STEP)
    new = master - LEARN_RATE * (
        first_hat / (jnp.sqrt(second_hat) + 1e-08) + DECAY_WEIGHT * master
    )
    return new, m1, m2


def update_kernel(elements, sq_ref, t_ref, ma_ref, m1_ref, m2_ref, em_ref, oma, om1, om2, oem, ow):
    core = lax.axis_index("c")
    sq = jnp.sum(jnp.sum(sq_ref[...], axis=0))
    sq = jnp.full((1, COLS), sq, F32)
    scale = jnp.minimum(1.0, 1.0 / jnp.sqrt(sq / elements + 1e-06))
    new, m1, m2 = adam(scale, from_piece(core, t_ref[...]), ma_ref[...], m1_ref[...], m2_ref[...])
    oma[...] = new
    om1[...] = m1
    om2[...] = m2
    oem[...] = EMA_KEEP * em_ref[...] + (1.0 - EMA_KEEP) * new
    ow[...] = jnp.broadcast_to(to_piece(core, new).astype(BF16)[None], ow.shape)


def place_kernel(w_ref, o_ref):
    for z in range(NZ):
        for x in range(X):
            at = (z * X + x) * GROUP
            a, b = w_ref.at[0, x, z], w_ref.at[1, x, z]
            o_ref[at : at + 8, :PC] = a[0:8]
            o_ref[at : at + 8, PC:] = a[8:16]
            o_ref[at + 16 : at + 24, :PC] = b[0:8]
            o_ref[at + 16 : at + 24, PC:] = b[8:16]
            p, q = a[16:24].astype(F32), b[16:24].astype(F32)
            left = jnp.where(upper(), p, q)
            right = pltpu.roll(jnp.where(upper(), q, p), 4, 0)
            o_ref[at + 8 : at + 16, :PC] = left.astype(BF16)
            o_ref[at + 8 : at + 16, PC:] = right.astype(BF16)


def place(w):
    rows = NZ * X * GROUP
    return pl.pallas_call(
        place_kernel,
        out_shape=jax.ShapeDtypeStruct((STEPS * rows, COLS), BF16),
        grid=(STEPS,),
        in_specs=[pl.BlockSpec((C, X, NZ, PR, PC), lambda i: (0, 0, i, 0, 0))],
        out_specs=pl.BlockSpec((rows, COLS), lambda i: (i, 0)),
        name="place",
    )(w)


def exchange(v, axes):
    return lax.all_to_all(v, axes, split_axis=0, concat_axis=0, tiled=True)


def copies(v, n):
    return jnp.broadcast_to(v[None], (n,) + v.shape)


def shards(grads, master, moment1, moment2, ema):
    local = grads[0]
    elements = local.shape[1] * local.shape[2] * T

    part = micro_sum(local)
    part = jnp.sum(exchange(part, "c"), axis=0)
    part = jnp.sum(exchange(part, "x"), axis=0)
    total = jnp.sum(exchange(part, "z"), axis=0)
    sq = jnp.sum((total * total).reshape(-1, 8, PC), axis=0)
    sq = jnp.sum(exchange(copies(sq, X * C * T), ("x", "c", "t")), axis=0)
    sq = exchange(copies(sq, Z), "z")

    state = jax.ShapeDtypeStruct((ROWS, COLS), F32)
    new_master, new_moment1, new_moment2, new_ema, w = pl.pallas_call(
        lambda *refs: update_kernel(elements, *refs),
        out_shape=(state, state, state, state, jax.ShapeDtypeStruct((Z, PR, PC), BF16)),
        name="update",
    )(sq, total, master, moment1, moment2, ema)

    w = exchange(w, "z")
    w = exchange(copies(w, X), "x")
    w = lax.all_gather(w, "c", axis=0, tiled=False)
    weights = place(w)
    return (new_master, new_moment1, new_moment2, new_ema, weights)


def solution(mesh):
    fine = Mesh(mesh.devices.reshape(Z, X, C, T), ("z", "x", "c", "t"))
    rows = ("z", "x", "c")
    return jax.shard_map(
        shards,
        mesh=fine,
        in_specs=(P(rows, None, None, "t"),) + (P(rows, "t"),) * 4,
        out_specs=(P(rows, "t"),) * 4 + (P(None, "t"),),
        check_vma=False,
    )
```

```python
import jax
import jax.numpy as jnp
from jax import lax
from jax.experimental import pallas as pl
from jax.experimental.pallas import tpu as pltpu
from jax.sharding import Mesh, PartitionSpec as P

STEP = 10
BETA_ONE = 0.9
BETA_TWO = 0.95
LEARN_RATE = 0.02
DECAY_WEIGHT = 0.1
EMA_KEEP = 0.99

Z, X, C, T = 16, 4, 2, 4
ROWS, COLS = 12, 256
PR, PC = 24, 128
GROUP = C * ROWS
STEPS = 2
NZ = Z // STEPS

F32 = jnp.float32
BF16 = jnp.bfloat16
F16 = jnp.float16

LIFT = 8.0


def upper():
    return lax.broadcasted_iota(jnp.int32, (8, PC), 0) < 4


def shared_tile(core, left, right):
    turned = pltpu.roll(right, 4, 0)
    return jnp.where(upper(), left, turned) if core == 0 else jnp.where(upper(), turned, left)


def to_piece(core, v):
    zero = [v[0:8, :PC], v[0:8, PC:], v[8:12, :PC], v[8:12, PC:]]
    one = [v[4:12, :PC], v[4:12, PC:], v[0:4, PC:], v[0:4, :PC]]
    return jnp.where(core == 0, jnp.concatenate(zero, axis=0), jnp.concatenate(one, axis=0))


def from_piece(core, p):
    full = jnp.concatenate([p[0:8], p[8:16]], axis=1)
    zero = jnp.concatenate([full, jnp.concatenate([p[16:20], p[20:24]], axis=1)], axis=0)
    one = jnp.concatenate([jnp.concatenate([p[20:24], p[16:20]], axis=1), full], axis=0)
    return jnp.where(core == 0, zero, one)


def sum_kernel(g_ref, o_ref):
    for z in range(NZ):
        for pair in range(X // 2):
            at = (z * X + 2 * pair) * GROUP
            v = g_ref[0, at : at + 2 * GROUP, :].astype(F32)
            for m in range(1, g_ref.shape[0]):
                v = v + g_ref[m, at : at + 2 * GROUP, :].astype(F32)
            for k in range(2):
                first, both, last = [v[k * GROUP + j : k * GROUP + j + 8] for j in (0, 8, 16)]
                for core, own in ((0, first), (1, last)):
                    o = o_ref.at[core, 2 * pair + k, z]
                    o[0:8] = own[:, :PC]
                    o[8:16] = own[:, PC:]
                    o[16:24] = shared_tile(core, both[:, :PC], both[:, PC:])


def micro_sum(local):
    rows = NZ * X * GROUP
    return pl.pallas_call(
        sum_kernel,
        out_shape=jax.ShapeDtypeStruct((C, X, Z, PR, PC), F32),
        grid=(STEPS,),
        in_specs=[pl.BlockSpec((local.shape[0], rows, COLS), lambda i: (0, i, 0))],
        out_specs=pl.BlockSpec((C, X, NZ, PR, PC), lambda i: (0, 0, i, 0, 0)),
        name="micro_sum",
    )(local)


def adam(scale, total, master, moment1, moment2):
    clipped = scale * total
    m1 = BETA_ONE * moment1 + (1.0 - BETA_ONE) * clipped
    m2 = BETA_TWO * moment2 + (1.0 - BETA_TWO) * clipped * clipped
    first_hat = m1 / (1.0 - BETA_ONE**STEP)
    second_hat = m2 / (1.0 - BETA_TWO**STEP)
    new = master - LEARN_RATE * (
        first_hat / (jnp.sqrt(second_hat) + 1e-08) + DECAY_WEIGHT * master
    )
    return new, m1, m2


def update_kernel(elements, sq_ref, t_ref, ma_ref, m1_ref, m2_ref, em_ref, oma, om1, om2, oem, ow):
    core = lax.axis_index("c")
    sq = jnp.sum(jnp.sum(sq_ref[...], axis=0))
    sq = jnp.full((1, COLS), sq, F32)
    scale = jnp.minimum(1.0, 1.0 / jnp.sqrt(sq / elements + 1e-06))
    new, m1, m2 = adam(scale, from_piece(core, t_ref[...]), ma_ref[...], m1_ref[...], m2_ref[...])
    oma[...] = new
    om1[...] = m1
    om2[...] = m2
    oem[...] = EMA_KEEP * em_ref[...] + (1.0 - EMA_KEEP) * new
    ow[...] = jnp.broadcast_to(to_piece(core, new).astype(BF16)[None], ow.shape)


def place_kernel(w_ref, o_ref):
    for z in range(NZ):
        for x in range(X):
            at = (z * X + x) * GROUP
            a, b = w_ref.at[0, x, z], w_ref.at[1, x, z]
            o_ref[at : at + 8, :PC] = a[0:8]
            o_ref[at : at + 8, PC:] = a[8:16]
            o_ref[at + 16 : at + 24, :PC] = b[0:8]
            o_ref[at + 16 : at + 24, PC:] = b[8:16]
            p, q = a[16:24].astype(F32), b[16:24].astype(F32)
            left = jnp.where(upper(), p, q)
            right = pltpu.roll(jnp.where(upper(), q, p), 4, 0)
            o_ref[at + 8 : at + 16, :PC] = left.astype(BF16)
            o_ref[at + 8 : at + 16, PC:] = right.astype(BF16)


def place(w):
    rows = NZ * X * GROUP
    return pl.pallas_call(
        place_kernel,
        out_shape=jax.ShapeDtypeStruct((STEPS * rows, COLS), BF16),
        grid=(STEPS,),
        in_specs=[pl.BlockSpec((C, X, NZ, PR, PC), lambda i: (0, 0, i, 0, 0))],
        out_specs=pl.BlockSpec((rows, COLS), lambda i: (i, 0)),
        name="place",
    )(w)


def exchange(v, axes):
    return lax.all_to_all(v, axes, split_axis=0, concat_axis=0, tiled=True)


def copies(v, n):
    return jnp.broadcast_to(v[None], (n,) + v.shape)


def shards(grads, master, moment1, moment2, ema):
    local = grads[0]
    elements = local.shape[1] * local.shape[2] * T

    part = micro_sum(local)
    part = jnp.sum(exchange(part, "c"), axis=0)
    part = jnp.sum(exchange(part, "x"), axis=0)
    part = exchange((part * LIFT).astype(F16), "z")
    total = jnp.sum(part.astype(F32), axis=0) * (1.0 / LIFT)
    sq = jnp.sum((total * total).reshape(-1, 8, PC), axis=0)
    sq = jnp.sum(exchange(copies(sq, X * C * T), ("x", "c", "t")), axis=0)
    sq = exchange(copies(sq, Z), "z")

    state = jax.ShapeDtypeStruct((ROWS, COLS), F32)
    new_master, new_moment1, new_moment2, new_ema, w = pl.pallas_call(
        lambda *refs: update_kernel(elements, *refs),
        out_shape=(state, state, state, state, jax.ShapeDtypeStruct((Z, PR, PC), BF16)),
        name="update",
    )(sq, total, master, moment1, moment2, ema)

    w = exchange(w, "z")
    w = exchange(copies(w, X), "x")
    w = lax.all_gather(w, "c", axis=0, tiled=False)
    weights = place(w)
    return (new_master, new_moment1, new_moment2, new_ema, weights)


def solution(mesh):
    fine = Mesh(mesh.devices.reshape(Z, X, C, T), ("z", "x", "c", "t"))
    rows = ("z", "x", "c")
    return jax.shard_map(
        shards,
        mesh=fine,
        in_specs=(P(rows, None, None, "t"),) + (P(rows, "t"),) * 4,
        out_specs=(P(rows, "t"),) * 4 + (P(None, "t"),),
        check_vma=False,
    )
```

```python
import jax
import jax.numpy as jnp
from jax import lax
from jax.experimental import pallas as pl
from jax.experimental.pallas import tpu as pltpu
from jax.sharding import Mesh, PartitionSpec as P

STEP = 10
BETA_ONE = 0.9
BETA_TWO = 0.95
LEARN_RATE = 0.02
DECAY_WEIGHT = 0.1
EMA_KEEP = 0.99

Z, X, C, T = 16, 4, 2, 4
ROWS, COLS = 12, 256
PR, PC = 24, 128
GROUP = C * ROWS
STEPS = 2
NZ = Z // STEPS
SUM_Z = 4

F32 = jnp.float32
BF16 = jnp.bfloat16


def upper():
    return lax.broadcasted_iota(jnp.int32, (8, PC), 0) < 4


def shared_tile(core, left, right):
    turned = pltpu.roll(right, 4, 0)
    return jnp.where(upper(), left, turned) if core == 0 else jnp.where(upper(), turned, left)


def to_piece(core, v):
    zero = [v[0:8, :PC], v[0:8, PC:], v[8:12, :PC], v[8:12, PC:]]
    one = [v[4:12, :PC], v[4:12, PC:], v[0:4, PC:], v[0:4, :PC]]
    return jnp.where(core == 0, jnp.concatenate(zero, axis=0), jnp.concatenate(one, axis=0))


def from_piece(core, p):
    full = jnp.concatenate([p[0:8], p[8:16]], axis=1)
    zero = jnp.concatenate([full, jnp.concatenate([p[16:20], p[20:24]], axis=1)], axis=0)
    one = jnp.concatenate([jnp.concatenate([p[20:24], p[16:20]], axis=1), full], axis=0)
    return jnp.where(core == 0, zero, one)


def sum_kernel(g_ref, o_ref):
    base = pl.program_id(0) * SUM_Z
    for z in range(SUM_Z):
        for pair in range(X // 2):
            at = (z * X + 2 * pair) * GROUP
            v = g_ref[0, at : at + 2 * GROUP, :].astype(F32)
            for m in range(1, g_ref.shape[0]):
                v = v + g_ref[m, at : at + 2 * GROUP, :].astype(F32)
            for k in range(2):
                first, both, last = [v[k * GROUP + j : k * GROUP + j + 8] for j in (0, 8, 16)]
                for core, own in ((0, first), (1, last)):
                    o = o_ref.at[core, 2 * pair + k, base + z]
                    o[0:8] = own[:, :PC]
                    o[8:16] = own[:, PC:]
                    o[16:24] = shared_tile(core, both[:, :PC], both[:, PC:])


def micro_sum(local):
    rows = SUM_Z * X * GROUP
    return pl.pallas_call(
        sum_kernel,
        out_shape=pltpu.VMEM((C, X, Z, PR, PC), F32),
        grid=(Z // SUM_Z,),
        in_specs=[pl.BlockSpec((local.shape[0], rows, COLS), lambda i: (0, i, 0))],
        out_specs=pl.BlockSpec(memory_space=pltpu.VMEM),
        name="micro_sum",
    )(local)


def adam(scale, total, master, moment1, moment2):
    clipped = scale * total
    m1 = BETA_ONE * moment1 + (1.0 - BETA_ONE) * clipped
    m2 = BETA_TWO * moment2 + (1.0 - BETA_TWO) * clipped * clipped
    first_hat = m1 / (1.0 - BETA_ONE**STEP)
    second_hat = m2 / (1.0 - BETA_TWO**STEP)
    new = master - LEARN_RATE * (
        first_hat / (jnp.sqrt(second_hat) + 1e-08) + DECAY_WEIGHT * master
    )
    return new, m1, m2


def update_kernel(elements, sq_ref, t_ref, ma_ref, m1_ref, m2_ref, em_ref, oma, om1, om2, oem, ow):
    core = lax.axis_index("c")
    sq = jnp.sum(jnp.sum(sq_ref[...], axis=0))
    sq = jnp.full((1, COLS), sq, F32)
    scale = jnp.minimum(1.0, 1.0 / jnp.sqrt(sq / elements + 1e-06))
    new, m1, m2 = adam(scale, from_piece(core, t_ref[...]), ma_ref[...], m1_ref[...], m2_ref[...])
    oma[...] = new
    om1[...] = m1
    om2[...] = m2
    oem[...] = EMA_KEEP * em_ref[...] + (1.0 - EMA_KEEP) * new
    ow[...] = jnp.broadcast_to(to_piece(core, new).astype(BF16)[None], ow.shape)


def place_kernel(w_ref, o_ref):
    base = pl.program_id(0) * NZ
    for z in range(NZ):
        for x in range(X):
            at = (z * X + x) * GROUP
            a, b = w_ref.at[0, x, base + z], w_ref.at[1, x, base + z]
            o_ref[at : at + 8, :PC] = a[0:8]
            o_ref[at : at + 8, PC:] = a[8:16]
            o_ref[at + 16 : at + 24, :PC] = b[0:8]
            o_ref[at + 16 : at + 24, PC:] = b[8:16]
            p, q = a[16:24].astype(F32), b[16:24].astype(F32)
            left = jnp.where(upper(), p, q)
            right = pltpu.roll(jnp.where(upper(), q, p), 4, 0)
            o_ref[at + 8 : at + 16, :PC] = left.astype(BF16)
            o_ref[at + 8 : at + 16, PC:] = right.astype(BF16)


def place(w):
    rows = NZ * X * GROUP
    return pl.pallas_call(
        place_kernel,
        out_shape=jax.ShapeDtypeStruct((STEPS * rows, COLS), BF16),
        grid=(STEPS,),
        in_specs=[pl.BlockSpec(memory_space=pltpu.VMEM)],
        out_specs=pl.BlockSpec((rows, COLS), lambda i: (i, 0)),
        name="place",
    )(*near(w))


def exchange(v, axes):
    return lax.all_to_all(v, axes, split_axis=0, concat_axis=0, tiled=True)


def near(*arrays):
    return [pltpu.with_memory_space_constraint(v, pltpu.VMEM) for v in arrays]


def copies(v, n):
    return jnp.broadcast_to(v[None], (n,) + v.shape)


def shards(grads, master, moment1, moment2, ema):
    local = grads[0]
    elements = local.shape[1] * local.shape[2] * T

    part = micro_sum(local)
    part = jnp.sum(exchange(part, "c"), axis=0)
    part = jnp.sum(exchange(part, "x"), axis=0)
    total = jnp.sum(exchange(part, "z"), axis=0)
    sq = jnp.sum((total * total).reshape(-1, 8, PC), axis=0)
    sq = jnp.sum(exchange(copies(sq, X * C * T), ("x", "c", "t")), axis=0)
    sq = exchange(copies(sq, Z), "z")

    state = pltpu.VMEM((ROWS, COLS), F32)
    whole = pl.BlockSpec(memory_space=pltpu.VMEM)
    new_master, new_moment1, new_moment2, new_ema, w = pl.pallas_call(
        lambda *refs: update_kernel(elements, *refs),
        out_shape=(state, state, state, state, pltpu.VMEM((Z, PR, PC), BF16)),
        in_specs=[whole] * 6,
        out_specs=(whole,) * 5,
        name="update",
    )(*near(sq, total, master, moment1, moment2, ema))

    w = exchange(w, "z")
    w = exchange(copies(w, X), "x")
    w = lax.all_gather(w, "c", axis=0, tiled=False)
    weights = place(w)
    return (new_master, new_moment1, new_moment2, new_ema, weights)


def solution(mesh):
    fine = Mesh(mesh.devices.reshape(Z, X, C, T), ("z", "x", "c", "t"))
    rows = ("z", "x", "c")
    return jax.shard_map(
        shards,
        mesh=fine,
        in_specs=(P(rows, None, None, "t"),) + (P(rows, "t"),) * 4,
        out_specs=(P(rows, "t"),) * 4 + (P(None, "t"),),
        check_vma=False,
    )
```

```python
import jax
import jax.numpy as jnp
from jax import lax
from jax.experimental import pallas as pl
from jax.experimental.pallas import tpu as pltpu
from jax.sharding import Mesh, PartitionSpec as P

STEP = 10
BETA_ONE = 0.9
BETA_TWO = 0.95
LEARN_RATE = 0.02
DECAY_WEIGHT = 0.1
EMA_KEEP = 0.99

Z, X, C, T = 16, 4, 2, 4
ROWS, COLS = 12, 256
PR, PC = 24, 128
GROUP = C * ROWS
STEPS = 2
NZ = Z // STEPS
SUM_Z = 4

F32 = jnp.float32
BF16 = jnp.bfloat16


def upper():
    return lax.broadcasted_iota(jnp.int32, (8, PC), 0) < 4


def shared_tile(core, left, right):
    turned = pltpu.roll(right, 4, 0)
    return jnp.where(upper(), left, turned) if core == 0 else jnp.where(upper(), turned, left)


def to_piece(core, v):
    zero = [v[0:8, :PC], v[0:8, PC:], v[8:12, :PC], v[8:12, PC:]]
    one = [v[4:12, :PC], v[4:12, PC:], v[0:4, PC:], v[0:4, :PC]]
    return jnp.where(core == 0, jnp.concatenate(zero, axis=0), jnp.concatenate(one, axis=0))


def from_piece(core, p):
    full = jnp.concatenate([p[0:8], p[8:16]], axis=1)
    zero = jnp.concatenate([full, jnp.concatenate([p[16:20], p[20:24]], axis=1)], axis=0)
    one = jnp.concatenate([jnp.concatenate([p[20:24], p[16:20]], axis=1), full], axis=0)
    return jnp.where(core == 0, zero, one)


def half_body(core, g_ref, o_ref):
    base = pl.program_id(0) * SUM_Z
    for z in range(SUM_Z):
        for x in range(X):
            at = (z * X + x) * GROUP + 8 * core
            v = g_ref[0, at : at + 16, :].astype(F32)
            for m in range(1, g_ref.shape[0]):
                v = v + g_ref[m, at : at + 16, :].astype(F32)
            own, both = (v[0:8], v[8:16]) if core == 0 else (v[8:16], v[0:8])
            o = o_ref.at[x, base + z]
            o[0:8] = own[:, :PC]
            o[8:16] = own[:, PC:]
            o[16:24] = shared_tile(core, both[:, :PC], both[:, PC:])


def half_kernel(own, g_ref, o_ref):
    me = lax.axis_index("c")
    core = me if own else 1 - me
    for k in range(C):
        pl.when(core == k)(lambda k=k: half_body(k, g_ref, o_ref))


def half_sum(local, own):
    rows = SUM_Z * X * GROUP
    return pl.pallas_call(
        lambda *refs: half_kernel(own, *refs),
        out_shape=pltpu.VMEM((X, Z, PR, PC), F32),
        grid=(Z // SUM_Z,),
        in_specs=[pl.BlockSpec((local.shape[0], rows, COLS), lambda i: (0, i, 0))],
        out_specs=pl.BlockSpec(memory_space=pltpu.VMEM),
        cost_estimate=pl.CostEstimate(flops=2_000_000, bytes_accessed=4_000_000, transcendentals=0),
        name="own_half" if own else "other_half",
    )(local)


def adam(scale, total, master, moment1, moment2):
    clipped = scale * total
    m1 = BETA_ONE * moment1 + (1.0 - BETA_ONE) * clipped
    m2 = BETA_TWO * moment2 + (1.0 - BETA_TWO) * clipped * clipped
    first_hat = m1 / (1.0 - BETA_ONE**STEP)
    second_hat = m2 / (1.0 - BETA_TWO**STEP)
    new = master - LEARN_RATE * (
        first_hat / (jnp.sqrt(second_hat) + 1e-08) + DECAY_WEIGHT * master
    )
    return new, m1, m2


def update_kernel(elements, sq_ref, t_ref, ma_ref, m1_ref, m2_ref, em_ref, oma, om1, om2, oem, ow):
    core = lax.axis_index("c")
    sq = jnp.sum(jnp.sum(sq_ref[...], axis=0))
    sq = jnp.full((1, COLS), sq, F32)
    scale = jnp.minimum(1.0, 1.0 / jnp.sqrt(sq / elements + 1e-06))
    new, m1, m2 = adam(scale, from_piece(core, t_ref[...]), ma_ref[...], m1_ref[...], m2_ref[...])
    oma[...] = new
    om1[...] = m1
    om2[...] = m2
    oem[...] = EMA_KEEP * em_ref[...] + (1.0 - EMA_KEEP) * new
    ow[...] = jnp.broadcast_to(to_piece(core, new).astype(BF16)[None], ow.shape)


def place_kernel(w_ref, o_ref):
    base = pl.program_id(0) * NZ
    for z in range(NZ):
        for x in range(X):
            at = (z * X + x) * GROUP
            a, b = w_ref.at[0, x, base + z], w_ref.at[1, x, base + z]
            o_ref[at : at + 8, :PC] = a[0:8]
            o_ref[at : at + 8, PC:] = a[8:16]
            o_ref[at + 16 : at + 24, :PC] = b[0:8]
            o_ref[at + 16 : at + 24, PC:] = b[8:16]
            p, q = a[16:24].astype(F32), b[16:24].astype(F32)
            left = jnp.where(upper(), p, q)
            right = pltpu.roll(jnp.where(upper(), q, p), 4, 0)
            o_ref[at + 8 : at + 16, :PC] = left.astype(BF16)
            o_ref[at + 8 : at + 16, PC:] = right.astype(BF16)


def place(w):
    rows = NZ * X * GROUP
    return pl.pallas_call(
        place_kernel,
        out_shape=jax.ShapeDtypeStruct((STEPS * rows, COLS), BF16),
        grid=(STEPS,),
        in_specs=[pl.BlockSpec(memory_space=pltpu.VMEM)],
        out_specs=pl.BlockSpec((rows, COLS), lambda i: (i, 0)),
        name="place",
    )(*near(w))


def exchange(v, axes):
    return lax.all_to_all(v, axes, split_axis=0, concat_axis=0, tiled=True)


def near(*arrays):
    return [pltpu.with_memory_space_constraint(v, pltpu.VMEM) for v in arrays]


def copies(v, n):
    return jnp.broadcast_to(v[None], (n,) + v.shape)


def shards(grads, master, moment1, moment2, ema):
    local = grads[0]
    elements = local.shape[1] * local.shape[2] * T

    other = lax.ppermute(half_sum(local, False), "c", [(0, 1), (1, 0)])
    part = half_sum(local, True) + other
    part = jnp.sum(exchange(part, "x"), axis=0)
    total = jnp.sum(exchange(part, "z"), axis=0)
    sq = jnp.sum(total * total, axis=0, keepdims=True)
    sq = jnp.sum(exchange(copies(sq, X * C * T), ("x", "c", "t")), axis=0)
    sq = exchange(copies(sq, Z), "z")

    state = pltpu.VMEM((ROWS, COLS), F32)
    whole = pl.BlockSpec(memory_space=pltpu.VMEM)
    new_master, new_moment1, new_moment2, new_ema, w = pl.pallas_call(
        lambda *refs: update_kernel(elements, *refs),
        out_shape=(state, state, state, state, pltpu.VMEM((Z, PR, PC), BF16)),
        in_specs=[whole] * 6,
        out_specs=(whole,) * 5,
        name="update",
    )(*near(sq, total, master, moment1, moment2, ema))

    w = exchange(w, "z")
    w = exchange(copies(w, X), "x")
    w = lax.all_gather(w, "c", axis=0, tiled=False)
    weights = place(w)
    return (new_master, new_moment1, new_moment2, new_ema, weights)


def solution(mesh):
    fine = Mesh(mesh.devices.reshape(Z, X, C, T), ("z", "x", "c", "t"))
    rows = ("z", "x", "c")
    return jax.shard_map(
        shards,
        mesh=fine,
        in_specs=(P(rows, None, None, "t"),) + (P(rows, "t"),) * 4,
        out_specs=(P(rows, "t"),) * 4 + (P(None, "t"),),
        check_vma=False,
    )
```

```python
import jax
import jax.numpy as jnp
from jax import lax
from jax.experimental import pallas as pl
from jax.experimental.pallas import tpu as pltpu
from jax.sharding import Mesh, PartitionSpec as P

STEP = 10
BETA_ONE = 0.9
BETA_TWO = 0.95
LEARN_RATE = 0.02
DECAY_WEIGHT = 0.1
EMA_KEEP = 0.99

Z, X, C, T = 16, 4, 2, 4
ROWS, COLS = 12, 256
PR, PC = 24, 128
GROUP = C * ROWS
STEPS = 2
NZ = Z // STEPS
SUM_Z = 4

F32 = jnp.float32
BF16 = jnp.bfloat16


def upper():
    return lax.broadcasted_iota(jnp.int32, (8, PC), 0) < 4


def shared_tile(core, left, right):
    turned = pltpu.roll(right, 4, 0)
    return jnp.where(upper(), left, turned) if core == 0 else jnp.where(upper(), turned, left)


def to_piece(core, v):
    zero = [v[0:8, :PC], v[0:8, PC:], v[8:12, :PC], v[8:12, PC:]]
    one = [v[4:12, :PC], v[4:12, PC:], v[0:4, PC:], v[0:4, :PC]]
    return jnp.where(core == 0, jnp.concatenate(zero, axis=0), jnp.concatenate(one, axis=0))


def from_piece(core, p):
    full = jnp.concatenate([p[0:8], p[8:16]], axis=1)
    zero = jnp.concatenate([full, jnp.concatenate([p[16:20], p[20:24]], axis=1)], axis=0)
    one = jnp.concatenate([jnp.concatenate([p[20:24], p[16:20]], axis=1), full], axis=0)
    return jnp.where(core == 0, zero, one)


def half_body(core, g_refs, o_ref):
    base = pl.program_id(0) * SUM_Z
    for z in range(SUM_Z):
        for x in range(X):
            at = (z * X + x) * GROUP + 8 * core
            v = sum(g_ref[0, at : at + 16, :].astype(F32) for g_ref in g_refs)
            own, both = (v[0:8], v[8:16]) if core == 0 else (v[8:16], v[0:8])
            o = o_ref.at[x, base + z]
            o[0:8] = own[:, :PC]
            o[8:16] = own[:, PC:]
            o[16:24] = shared_tile(core, both[:, :PC], both[:, PC:])


def half_kernel(own, *refs):
    me = lax.axis_index("c")
    core = me if own else 1 - me
    for k in range(C):
        pl.when(core == k)(lambda k=k: half_body(k, refs[:-1], refs[-1]))


def half_sum(local, own):
    rows = SUM_Z * X * GROUP
    return pl.pallas_call(
        lambda *refs: half_kernel(own, *refs),
        out_shape=pltpu.VMEM((X, Z, PR, PC), F32),
        grid=(Z // SUM_Z,),
        in_specs=[
            pl.BlockSpec((1, rows, COLS), lambda i, m=m: (m, i, 0)) for m in range(local.shape[0])
        ],
        out_specs=pl.BlockSpec(memory_space=pltpu.VMEM),
        cost_estimate=pl.CostEstimate(flops=2_000_000, bytes_accessed=4_000_000, transcendentals=0),
        name="own_half" if own else "other_half",
    )(*[local] * local.shape[0])


def adam(scale, total, master, moment1, moment2):
    clipped = scale * total
    m1 = BETA_ONE * moment1 + (1.0 - BETA_ONE) * clipped
    m2 = BETA_TWO * moment2 + (1.0 - BETA_TWO) * clipped * clipped
    first_hat = m1 / (1.0 - BETA_ONE**STEP)
    second_hat = m2 / (1.0 - BETA_TWO**STEP)
    new = master - LEARN_RATE * (
        first_hat / (jnp.sqrt(second_hat) + 1e-08) + DECAY_WEIGHT * master
    )
    return new, m1, m2


def update_kernel(elements, sq_ref, t_ref, ma_ref, m1_ref, m2_ref, em_ref, oma, om1, om2, oem, ow):
    core = lax.axis_index("c")
    sq = jnp.sum(jnp.sum(sq_ref[...], axis=0))
    sq = jnp.full((1, COLS), sq, F32)
    scale = jnp.minimum(1.0, 1.0 / jnp.sqrt(sq / elements + 1e-06))
    new, m1, m2 = adam(scale, from_piece(core, t_ref[...]), ma_ref[...], m1_ref[...], m2_ref[...])
    oma[...] = new
    om1[...] = m1
    om2[...] = m2
    oem[...] = EMA_KEEP * em_ref[...] + (1.0 - EMA_KEEP) * new
    ow[...] = jnp.broadcast_to(to_piece(core, new).astype(BF16)[None], ow.shape)


def place_kernel(w_ref, o_ref):
    base = pl.program_id(0) * NZ
    for z in range(NZ):
        for x in range(X):
            at = (z * X + x) * GROUP
            a, b = w_ref.at[0, x, base + z], w_ref.at[1, x, base + z]
            o_ref[at : at + 8, :PC] = a[0:8]
            o_ref[at : at + 8, PC:] = a[8:16]
            o_ref[at + 16 : at + 24, :PC] = b[0:8]
            o_ref[at + 16 : at + 24, PC:] = b[8:16]
            p, q = a[16:24].astype(F32), b[16:24].astype(F32)
            left = jnp.where(upper(), p, q)
            right = pltpu.roll(jnp.where(upper(), q, p), 4, 0)
            o_ref[at + 8 : at + 16, :PC] = left.astype(BF16)
            o_ref[at + 8 : at + 16, PC:] = right.astype(BF16)


def place(w):
    rows = NZ * X * GROUP
    return pl.pallas_call(
        place_kernel,
        out_shape=jax.ShapeDtypeStruct((STEPS * rows, COLS), BF16),
        grid=(STEPS,),
        in_specs=[pl.BlockSpec(memory_space=pltpu.VMEM)],
        out_specs=pl.BlockSpec((rows, COLS), lambda i: (i, 0)),
        name="place",
    )(*near(w))


def exchange(v, axes):
    return lax.all_to_all(v, axes, split_axis=0, concat_axis=0, tiled=True)


def near(*arrays):
    return [pltpu.with_memory_space_constraint(v, pltpu.VMEM) for v in arrays]


def copies(v, n):
    return jnp.broadcast_to(v[None], (n,) + v.shape)


def shards(grads, master, moment1, moment2, ema):
    local = grads[0]
    elements = local.shape[1] * local.shape[2] * T

    other = lax.ppermute(half_sum(local, False), "c", [(0, 1), (1, 0)])
    part = half_sum(local, True) + other
    part = jnp.sum(exchange(part, "x"), axis=0)
    total = jnp.sum(exchange(part, "z"), axis=0)
    sq = jnp.sum(total * total, axis=0, keepdims=True)
    sq = jnp.sum(exchange(copies(sq, X * C * T), ("x", "c", "t")), axis=0)
    sq = exchange(copies(sq, Z), "z")

    state = jax.ShapeDtypeStruct((ROWS, COLS), F32)
    whole = pl.BlockSpec(memory_space=pltpu.VMEM)
    new_master, new_moment1, new_moment2, new_ema, w = pl.pallas_call(
        lambda *refs: update_kernel(elements, *refs),
        out_shape=(state, state, state, state, pltpu.VMEM((Z, PR, PC), BF16)),
        in_specs=[whole] * 6,
        out_specs=(pl.BlockSpec(),) * 4 + (whole,),
        name="update",
    )(*near(sq, total, master, moment1, moment2, ema))

    w = exchange(w, "z")
    w = exchange(copies(w, X), "x")
    w = lax.all_gather(w, "c", axis=0, tiled=False)
    weights = place(w)
    return (new_master, new_moment1, new_moment2, new_ema, weights)


def solution(mesh):
    fine = Mesh(mesh.devices.reshape(Z, X, C, T), ("z", "x", "c", "t"))
    rows = ("z", "x", "c")
    return jax.shard_map(
        shards,
        mesh=fine,
        in_specs=(P(rows, None, None, "t"),) + (P(rows, "t"),) * 4,
        out_specs=(P(rows, "t"),) * 4 + (P(None, "t"),),
        check_vma=False,
    )
```

```python
import jax
import jax.numpy as jnp
from jax import lax
from jax.experimental import pallas as pl
from jax.experimental.pallas import tpu as pltpu
from jax.sharding import Mesh, PartitionSpec as P

STEP = 10
BETA_ONE = 0.9
BETA_TWO = 0.95
LEARN_RATE = 0.02
DECAY_WEIGHT = 0.1
EMA_KEEP = 0.99

Z, X, C, T = 16, 4, 2, 4
ROWS, COLS = 12, 256
PR, PC = 24, 128
GROUP = C * ROWS
STEPS = 2
NZ = Z // STEPS
SUM_Z = 4

F32 = jnp.float32
BF16 = jnp.bfloat16
F16 = jnp.float16

LIFT = 32.0


def upper():
    return lax.broadcasted_iota(jnp.int32, (8, PC), 0) < 4


def shared_tile(core, left, right):
    turned = pltpu.roll(right, 4, 0)
    return jnp.where(upper(), left, turned) if core == 0 else jnp.where(upper(), turned, left)


def to_piece(core, v):
    zero = [v[0:8, :PC], v[0:8, PC:], v[8:12, :PC], v[8:12, PC:]]
    one = [v[4:12, :PC], v[4:12, PC:], v[0:4, PC:], v[0:4, :PC]]
    return jnp.where(core == 0, jnp.concatenate(zero, axis=0), jnp.concatenate(one, axis=0))


def from_piece(core, p):
    full = jnp.concatenate([p[0:8], p[8:16]], axis=1)
    zero = jnp.concatenate([full, jnp.concatenate([p[16:20], p[20:24]], axis=1)], axis=0)
    one = jnp.concatenate([jnp.concatenate([p[20:24], p[16:20]], axis=1), full], axis=0)
    return jnp.where(core == 0, zero, one)


def half_body(core, g_refs, o_ref):
    base = pl.program_id(0) * SUM_Z
    for z in range(SUM_Z):
        for x in range(X):
            at = (z * X + x) * GROUP + 8 * core
            v = sum(g_ref[0, at : at + 16, :].astype(F32) for g_ref in g_refs)
            own, both = (v[0:8], v[8:16]) if core == 0 else (v[8:16], v[0:8])
            o = o_ref.at[x, base + z]
            o[0:8] = own[:, :PC]
            o[8:16] = own[:, PC:]
            o[16:24] = shared_tile(core, both[:, :PC], both[:, PC:])


def half_kernel(own, *refs):
    me = lax.axis_index("c")
    core = me if own else 1 - me
    for k in range(C):
        pl.when(core == k)(lambda k=k: half_body(k, refs[:-1], refs[-1]))


def half_sum(local, own):
    rows = SUM_Z * X * GROUP
    return pl.pallas_call(
        lambda *refs: half_kernel(own, *refs),
        out_shape=pltpu.VMEM((X, Z, PR, PC), F32),
        grid=(Z // SUM_Z,),
        in_specs=[
            pl.BlockSpec((1, rows, COLS), lambda i, m=m: (m, i, 0)) for m in range(local.shape[0])
        ],
        out_specs=pl.BlockSpec(memory_space=pltpu.VMEM),
        cost_estimate=pl.CostEstimate(flops=2_000_000, bytes_accessed=4_000_000, transcendentals=0),
        name="own_half" if own else "other_half",
    )(*[local] * local.shape[0])


def adam(scale, total, master, moment1, moment2):
    clipped = scale * total
    m1 = BETA_ONE * moment1 + (1.0 - BETA_ONE) * clipped
    m2 = BETA_TWO * moment2 + (1.0 - BETA_TWO) * clipped * clipped
    first_hat = m1 / (1.0 - BETA_ONE**STEP)
    second_hat = m2 / (1.0 - BETA_TWO**STEP)
    new = master - LEARN_RATE * (
        first_hat / (jnp.sqrt(second_hat) + 1e-08) + DECAY_WEIGHT * master
    )
    return new, m1, m2


def update_kernel(elements, sq_ref, t_ref, ma_ref, m1_ref, m2_ref, em_ref, oma, om1, om2, oem, ow):
    core = lax.axis_index("c")
    sq = jnp.sum(jnp.sum(sq_ref[...], axis=0))
    sq = jnp.full((1, COLS), sq, F32)
    scale = jnp.minimum(1.0, 1.0 / jnp.sqrt(sq / elements + 1e-06))
    new, m1, m2 = adam(scale, from_piece(core, t_ref[...]), ma_ref[...], m1_ref[...], m2_ref[...])
    oma[...] = new
    om1[...] = m1
    om2[...] = m2
    oem[...] = EMA_KEEP * em_ref[...] + (1.0 - EMA_KEEP) * new
    ow[...] = jnp.broadcast_to(to_piece(core, new).astype(BF16)[None], ow.shape)


def place_kernel(w_ref, o_ref):
    base = pl.program_id(0) * NZ
    for z in range(NZ):
        for x in range(X):
            at = (z * X + x) * GROUP
            a, b = w_ref.at[0, x, base + z], w_ref.at[1, x, base + z]
            o_ref[at : at + 8, :PC] = a[0:8]
            o_ref[at : at + 8, PC:] = a[8:16]
            o_ref[at + 16 : at + 24, :PC] = b[0:8]
            o_ref[at + 16 : at + 24, PC:] = b[8:16]
            p, q = a[16:24].astype(F32), b[16:24].astype(F32)
            left = jnp.where(upper(), p, q)
            right = pltpu.roll(jnp.where(upper(), q, p), 4, 0)
            o_ref[at + 8 : at + 16, :PC] = left.astype(BF16)
            o_ref[at + 8 : at + 16, PC:] = right.astype(BF16)


def place(w):
    rows = NZ * X * GROUP
    return pl.pallas_call(
        place_kernel,
        out_shape=jax.ShapeDtypeStruct((STEPS * rows, COLS), BF16),
        grid=(STEPS,),
        in_specs=[pl.BlockSpec(memory_space=pltpu.VMEM)],
        out_specs=pl.BlockSpec((rows, COLS), lambda i: (i, 0)),
        name="place",
    )(*near(w))


def exchange(v, axes):
    return lax.all_to_all(v, axes, split_axis=0, concat_axis=0, tiled=True)


def near(*arrays):
    return [pltpu.with_memory_space_constraint(v, pltpu.VMEM) for v in arrays]


def copies(v, n):
    return jnp.broadcast_to(v[None], (n,) + v.shape)


def shards(grads, master, moment1, moment2, ema):
    local = grads[0]
    elements = local.shape[1] * local.shape[2] * T

    other = lax.ppermute(half_sum(local, False), "c", [(0, 1), (1, 0)])
    part = half_sum(local, True) + other
    part = exchange((part * LIFT).astype(F16), "x")
    part = jnp.sum(part.astype(F32), axis=0) * (1.0 / LIFT)
    total = jnp.sum(exchange(part, "z"), axis=0)
    sq = jnp.sum(total * total, axis=0, keepdims=True)
    sq = jnp.sum(exchange(copies(sq, X * C * T), ("x", "c", "t")), axis=0)
    sq = exchange(copies(sq, Z), "z")

    state = jax.ShapeDtypeStruct((ROWS, COLS), F32)
    whole = pl.BlockSpec(memory_space=pltpu.VMEM)
    new_master, new_moment1, new_moment2, new_ema, w = pl.pallas_call(
        lambda *refs: update_kernel(elements, *refs),
        out_shape=(state, state, state, state, pltpu.VMEM((Z, PR, PC), BF16)),
        in_specs=[whole] * 6,
        out_specs=(pl.BlockSpec(),) * 4 + (whole,),
        name="update",
    )(*near(sq, total, master, moment1, moment2, ema))

    w = exchange(w, "z")
    w = exchange(copies(w, X), "x")
    w = lax.all_gather(w, "c", axis=0, tiled=False)
    weights = place(w)
    return (new_master, new_moment1, new_moment2, new_ema, weights)


def solution(mesh):
    fine = Mesh(mesh.devices.reshape(Z, X, C, T), ("z", "x", "c", "t"))
    rows = ("z", "x", "c")
    return jax.shard_map(
        shards,
        mesh=fine,
        in_specs=(P(rows, None, None, "t"),) + (P(rows, "t"),) * 4,
        out_specs=(P(rows, "t"),) * 4 + (P(None, "t"),),
        check_vma=False,
    )
```

```python
import jax
import jax.numpy as jnp
from jax import lax
from jax.experimental import pallas as pl
from jax.experimental.pallas import tpu as pltpu
from jax.sharding import Mesh, PartitionSpec as P

STEP = 10
BETA_ONE = 0.9
BETA_TWO = 0.95
LEARN_RATE = 0.02
DECAY_WEIGHT = 0.1
EMA_KEEP = 0.99

Z, X, C, T = 16, 4, 2, 4
ROWS, COLS = 12, 256
PR, PC = 24, 128
GROUP = C * ROWS
STEPS = 2
NZ = Z // STEPS
SUM_Z = 4

F32 = jnp.float32
BF16 = jnp.bfloat16
F16 = jnp.float16

LIFT = 32.0


def upper():
    return lax.broadcasted_iota(jnp.int32, (8, PC), 0) < 4


def shared_tile(core, left, right):
    turned = pltpu.roll(right, 4, 0)
    return jnp.where(upper(), left, turned) if core == 0 else jnp.where(upper(), turned, left)


def to_piece(core, v):
    zero = [v[0:8, :PC], v[0:8, PC:], v[8:12, :PC], v[8:12, PC:]]
    one = [v[4:12, :PC], v[4:12, PC:], v[0:4, PC:], v[0:4, :PC]]
    return jnp.where(core == 0, jnp.concatenate(zero, axis=0), jnp.concatenate(one, axis=0))


def from_piece(core, p):
    full = jnp.concatenate([p[0:8], p[8:16]], axis=1)
    zero = jnp.concatenate([full, jnp.concatenate([p[16:20], p[20:24]], axis=1)], axis=0)
    one = jnp.concatenate([jnp.concatenate([p[20:24], p[16:20]], axis=1), full], axis=0)
    return jnp.where(core == 0, zero, one)


def sum_body(me, g_ref, own_ref, other_ref):
    base = pl.program_id(0) * SUM_Z
    refs = (own_ref, other_ref) if me == 0 else (other_ref, own_ref)
    for z in range(SUM_Z):
        for pair in range(X // 2):
            at = (z * X + 2 * pair) * GROUP
            v = g_ref[0, at : at + 2 * GROUP, :].astype(F32)
            for m in range(1, g_ref.shape[0]):
                v = v + g_ref[m, at : at + 2 * GROUP, :].astype(F32)
            for k in range(2):
                first, both, last = [v[k * GROUP + j : k * GROUP + j + 8] for j in (0, 8, 16)]
                for core, owned in ((0, first), (1, last)):
                    o = refs[core].at[2 * pair + k, base + z]
                    o[0:8] = owned[:, :PC]
                    o[8:16] = owned[:, PC:]
                    o[16:24] = shared_tile(core, both[:, :PC], both[:, PC:])


def sum_kernel(*refs):
    me = lax.axis_index("c")
    for k in range(C):
        pl.when(me == k)(lambda k=k: sum_body(k, *refs))


def micro_sum(local):
    rows = SUM_Z * X * GROUP
    return pl.pallas_call(
        sum_kernel,
        out_shape=(pltpu.VMEM((X, Z, PR, PC), F32),) * 2,
        grid=(Z // SUM_Z,),
        in_specs=[pl.BlockSpec((local.shape[0], rows, COLS), lambda i: (0, i, 0))],
        out_specs=(pl.BlockSpec(memory_space=pltpu.VMEM),) * 2,
        name="micro_sum",
    )(local)


def adam(scale, total, master, moment1, moment2):
    clipped = scale * total
    m1 = BETA_ONE * moment1 + (1.0 - BETA_ONE) * clipped
    m2 = BETA_TWO * moment2 + (1.0 - BETA_TWO) * clipped * clipped
    first_hat = m1 / (1.0 - BETA_ONE**STEP)
    second_hat = m2 / (1.0 - BETA_TWO**STEP)
    new = master - LEARN_RATE * (
        first_hat / (jnp.sqrt(second_hat) + 1e-08) + DECAY_WEIGHT * master
    )
    return new, m1, m2


def update_kernel(elements, sq_ref, t_ref, ma_ref, m1_ref, m2_ref, em_ref, oma, om1, om2, oem, ow):
    core = lax.axis_index("c")
    sq = jnp.sum(jnp.sum(sq_ref[...], axis=0))
    sq = jnp.full((1, COLS), sq, F32)
    scale = jnp.minimum(1.0, 1.0 / jnp.sqrt(sq / elements + 1e-06))
    new, m1, m2 = adam(scale, from_piece(core, t_ref[...]), ma_ref[...], m1_ref[...], m2_ref[...])
    oma[...] = new
    om1[...] = m1
    om2[...] = m2
    oem[...] = EMA_KEEP * em_ref[...] + (1.0 - EMA_KEEP) * new
    ow[...] = jnp.broadcast_to(to_piece(core, new).astype(BF16)[None], ow.shape)


def place_kernel(w_ref, o_ref):
    base = pl.program_id(0) * NZ
    for z in range(NZ):
        for x in range(X):
            at = (z * X + x) * GROUP
            a, b = w_ref.at[0, x, base + z], w_ref.at[1, x, base + z]
            o_ref[at : at + 8, :PC] = a[0:8]
            o_ref[at : at + 8, PC:] = a[8:16]
            o_ref[at + 16 : at + 24, :PC] = b[0:8]
            o_ref[at + 16 : at + 24, PC:] = b[8:16]
            p, q = a[16:24].astype(F32), b[16:24].astype(F32)
            left = jnp.where(upper(), p, q)
            right = pltpu.roll(jnp.where(upper(), q, p), 4, 0)
            o_ref[at + 8 : at + 16, :PC] = left.astype(BF16)
            o_ref[at + 8 : at + 16, PC:] = right.astype(BF16)


def place(w):
    rows = NZ * X * GROUP
    return pl.pallas_call(
        place_kernel,
        out_shape=jax.ShapeDtypeStruct((STEPS * rows, COLS), BF16),
        grid=(STEPS,),
        in_specs=[pl.BlockSpec(memory_space=pltpu.VMEM)],
        out_specs=pl.BlockSpec((rows, COLS), lambda i: (i, 0)),
        name="place",
    )(*near(w))


def exchange(v, axes):
    return lax.all_to_all(v, axes, split_axis=0, concat_axis=0, tiled=True)


def near(*arrays):
    return [pltpu.with_memory_space_constraint(v, pltpu.VMEM) for v in arrays]


def copies(v, n):
    return jnp.broadcast_to(v[None], (n,) + v.shape)


def shards(grads, master, moment1, moment2, ema):
    local = grads[0]
    elements = local.shape[1] * local.shape[2] * T

    part, other = micro_sum(local)
    part = part + lax.ppermute(other, "c", [(0, 1), (1, 0)])
    part = exchange((part * LIFT).astype(F16), "x")
    part = jnp.sum(part.astype(F32), axis=0) * (1.0 / LIFT)
    total = jnp.sum(exchange(part, "z"), axis=0)
    sq = jnp.sum(total * total, axis=0, keepdims=True)
    sq = jnp.sum(exchange(copies(sq, X * C * T), ("x", "c", "t")), axis=0)
    sq = exchange(copies(sq, Z), "z")

    state = jax.ShapeDtypeStruct((ROWS, COLS), F32)
    whole = pl.BlockSpec(memory_space=pltpu.VMEM)
    new_master, new_moment1, new_moment2, new_ema, w = pl.pallas_call(
        lambda *refs: update_kernel(elements, *refs),
        out_shape=(state, state, state, state, pltpu.VMEM((Z, PR, PC), BF16)),
        in_specs=[whole] * 6,
        out_specs=(pl.BlockSpec(),) * 4 + (whole,),
        name="update",
    )(*near(sq, total, master, moment1, moment2, ema))

    w = exchange(w, "z")
    w = exchange(copies(w, X), "x")
    w = lax.all_gather(w, "c", axis=0, tiled=False)
    weights = place(w)
    return (new_master, new_moment1, new_moment2, new_ema, weights)


def solution(mesh):
    fine = Mesh(mesh.devices.reshape(Z, X, C, T), ("z", "x", "c", "t"))
    rows = ("z", "x", "c")
    return jax.shard_map(
        shards,
        mesh=fine,
        in_specs=(P(rows, None, None, "t"),) + (P(rows, "t"),) * 4,
        out_specs=(P(rows, "t"),) * 4 + (P(None, "t"),),
        check_vma=False,
    )
```

```python
import jax
import jax.numpy as jnp
from jax import lax
from jax.experimental import pallas as pl
from jax.experimental.pallas import tpu as pltpu
from jax.sharding import Mesh, PartitionSpec as P

STEP = 10
BETA_ONE = 0.9
BETA_TWO = 0.95
LEARN_RATE = 0.02
DECAY_WEIGHT = 0.1
EMA_KEEP = 0.99

Z, X, C, T = 16, 4, 2, 4
ROWS, COLS = 12, 256
PR, PC = 24, 128
GROUP = C * ROWS
STEPS = 2
NZ = Z // STEPS
SUM_Z = 8

F32 = jnp.float32
BF16 = jnp.bfloat16
F16 = jnp.float16

LIFT = 32.0


def upper():
    return lax.broadcasted_iota(jnp.int32, (8, PC), 0) < 4


def shared_tile(core, left, right):
    turned = pltpu.roll(right, 4, 0)
    return jnp.where(upper(), left, turned) if core == 0 else jnp.where(upper(), turned, left)


def to_piece(core, v):
    zero = [v[0:8, :PC], v[0:8, PC:], v[8:12, :PC], v[8:12, PC:]]
    one = [v[4:12, :PC], v[4:12, PC:], v[0:4, PC:], v[0:4, :PC]]
    return jnp.where(core == 0, jnp.concatenate(zero, axis=0), jnp.concatenate(one, axis=0))


def from_piece(core, p):
    full = jnp.concatenate([p[0:8], p[8:16]], axis=1)
    zero = jnp.concatenate([full, jnp.concatenate([p[16:20], p[20:24]], axis=1)], axis=0)
    one = jnp.concatenate([jnp.concatenate([p[20:24], p[16:20]], axis=1), full], axis=0)
    return jnp.where(core == 0, zero, one)


def sum_body(me, g_ref, own_ref, other_ref):
    base = pl.program_id(0) * SUM_Z
    refs = (own_ref, other_ref) if me == 0 else (other_ref, own_ref)
    for z in range(SUM_Z):
        for pair in range(X // 2):
            at = (z * X + 2 * pair) * GROUP
            v = g_ref[0, at : at + 2 * GROUP, :].astype(F32)
            for m in range(1, g_ref.shape[0]):
                v = v + g_ref[m, at : at + 2 * GROUP, :].astype(F32)
            for k in range(2):
                first, both, last = [v[k * GROUP + j : k * GROUP + j + 8] for j in (0, 8, 16)]
                for core, owned in ((0, first), (1, last)):
                    o = refs[core].at[2 * pair + k, base + z]
                    o[0:8] = owned[:, :PC]
                    o[8:16] = owned[:, PC:]
                    o[16:24] = shared_tile(core, both[:, :PC], both[:, PC:])


def sum_kernel(*refs):
    me = lax.axis_index("c")
    for k in range(C):
        pl.when(me == k)(lambda k=k: sum_body(k, *refs))


def micro_sum(local):
    rows = SUM_Z * X * GROUP
    return pl.pallas_call(
        sum_kernel,
        out_shape=(pltpu.VMEM((X, Z, PR, PC), F32),) * 2,
        grid=(Z // SUM_Z,),
        in_specs=[pl.BlockSpec((local.shape[0], rows, COLS), lambda i: (0, i, 0))],
        out_specs=(pl.BlockSpec(memory_space=pltpu.VMEM),) * 2,
        name="micro_sum",
    )(local)


def adam(scale, total, master, moment1, moment2):
    clipped = scale * total
    m1 = BETA_ONE * moment1 + (1.0 - BETA_ONE) * clipped
    m2 = BETA_TWO * moment2 + (1.0 - BETA_TWO) * clipped * clipped
    first_hat = m1 / (1.0 - BETA_ONE**STEP)
    second_hat = m2 / (1.0 - BETA_TWO**STEP)
    new = master - LEARN_RATE * (
        first_hat / (jnp.sqrt(second_hat) + 1e-08) + DECAY_WEIGHT * master
    )
    return new, m1, m2


def update_kernel(elements, sq_ref, t_ref, ma_ref, m1_ref, m2_ref, em_ref, oma, om1, om2, oem, ow):
    core = lax.axis_index("c")
    sq = jnp.sum(jnp.sum(sq_ref[...], axis=0))
    sq = jnp.full((1, COLS), sq, F32)
    scale = jnp.minimum(1.0, 1.0 / jnp.sqrt(sq / elements + 1e-06))
    new, m1, m2 = adam(scale, from_piece(core, t_ref[...]), ma_ref[...], m1_ref[...], m2_ref[...])
    oma[...] = new
    om1[...] = m1
    om2[...] = m2
    oem[...] = EMA_KEEP * em_ref[...] + (1.0 - EMA_KEEP) * new
    ow[...] = jnp.broadcast_to(to_piece(core, new).astype(BF16)[None], ow.shape)


def place_kernel(w_ref, o_ref):
    base = pl.program_id(0) * NZ
    for z in range(NZ):
        for x in range(X):
            at = (z * X + x) * GROUP
            a, b = w_ref.at[0, x, base + z], w_ref.at[1, x, base + z]
            o_ref[at : at + 8, :PC] = a[0:8]
            o_ref[at : at + 8, PC:] = a[8:16]
            o_ref[at + 16 : at + 24, :PC] = b[0:8]
            o_ref[at + 16 : at + 24, PC:] = b[8:16]
            p, q = a[16:24].astype(F32), b[16:24].astype(F32)
            left = jnp.where(upper(), p, q)
            right = pltpu.roll(jnp.where(upper(), q, p), 4, 0)
            o_ref[at + 8 : at + 16, :PC] = left.astype(BF16)
            o_ref[at + 8 : at + 16, PC:] = right.astype(BF16)


def place(w):
    rows = NZ * X * GROUP
    return pl.pallas_call(
        place_kernel,
        out_shape=jax.ShapeDtypeStruct((STEPS * rows, COLS), BF16),
        grid=(STEPS,),
        in_specs=[pl.BlockSpec(memory_space=pltpu.VMEM)],
        out_specs=pl.BlockSpec((rows, COLS), lambda i: (i, 0)),
        name="place",
    )(*near(w))


def exchange(v, axes):
    return lax.all_to_all(v, axes, split_axis=0, concat_axis=0, tiled=True)


def near(*arrays):
    return [pltpu.with_memory_space_constraint(v, pltpu.VMEM) for v in arrays]


def copies(v, n):
    return jnp.broadcast_to(v[None], (n,) + v.shape)


def shards(grads, master, moment1, moment2, ema):
    local = grads[0]
    elements = local.shape[1] * local.shape[2] * T

    part, other = micro_sum(local)
    part = part + lax.ppermute(other, "c", [(0, 1), (1, 0)])
    part = exchange((part * LIFT).astype(F16), "x")
    part = jnp.sum(part.astype(F32), axis=0) * (1.0 / LIFT)
    total = jnp.sum(exchange(part, "z"), axis=0)
    sq = jnp.sum(total * total, axis=0, keepdims=True)
    sq = jnp.sum(exchange(copies(sq, X * C * T), ("x", "c", "t")), axis=0)
    sq = exchange(copies(sq, Z), "z")

    state = jax.ShapeDtypeStruct((ROWS, COLS), F32)
    whole = pl.BlockSpec(memory_space=pltpu.VMEM)
    new_master, new_moment1, new_moment2, new_ema, w = pl.pallas_call(
        lambda *refs: update_kernel(elements, *refs),
        out_shape=(state, state, state, state, pltpu.VMEM((Z, PR, PC), BF16)),
        in_specs=[whole] * 6,
        out_specs=(pl.BlockSpec(),) * 4 + (whole,),
        name="update",
    )(*near(sq, total, master, moment1, moment2, ema))

    w = exchange(w, "z")
    w = exchange(copies(w, X), "x")
    w = lax.all_gather(w, "c", axis=0, tiled=False)
    weights = place(w)
    return (new_master, new_moment1, new_moment2, new_ema, weights)


def solution(mesh):
    fine = Mesh(mesh.devices.reshape(Z, X, C, T), ("z", "x", "c", "t"))
    rows = ("z", "x", "c")
    return jax.shard_map(
        shards,
        mesh=fine,
        in_specs=(P(rows, None, None, "t"),) + (P(rows, "t"),) * 4,
        out_specs=(P(rows, "t"),) * 4 + (P(None, "t"),),
        check_vma=False,
    )
```

```python
import jax
import jax.numpy as jnp
from jax import lax
from jax.experimental import pallas as pl
from jax.experimental.pallas import tpu as pltpu
from jax.sharding import Mesh, PartitionSpec as P

STEP = 10
BETA_ONE = 0.9
BETA_TWO = 0.95
LEARN_RATE = 0.02
DECAY_WEIGHT = 0.1
EMA_KEEP = 0.99

Z, X, C, T = 16, 4, 2, 4
ROWS, COLS = 12, 256
PR, PC = 24, 128
GROUP = C * ROWS
STEPS = 2
NZ = Z // STEPS
SUM_Z = 16

F32 = jnp.float32
BF16 = jnp.bfloat16
F16 = jnp.float16

LIFT = 32.0


def upper():
    return lax.broadcasted_iota(jnp.int32, (8, PC), 0) < 4


def shared_tile(core, left, right):
    turned = pltpu.roll(right, 4, 0)
    return jnp.where(upper(), left, turned) if core == 0 else jnp.where(upper(), turned, left)


def to_piece(core, v):
    zero = [v[0:8, :PC], v[0:8, PC:], v[8:12, :PC], v[8:12, PC:]]
    one = [v[4:12, :PC], v[4:12, PC:], v[0:4, PC:], v[0:4, :PC]]
    return jnp.where(core == 0, jnp.concatenate(zero, axis=0), jnp.concatenate(one, axis=0))


def from_piece(core, p):
    full = jnp.concatenate([p[0:8], p[8:16]], axis=1)
    zero = jnp.concatenate([full, jnp.concatenate([p[16:20], p[20:24]], axis=1)], axis=0)
    one = jnp.concatenate([jnp.concatenate([p[20:24], p[16:20]], axis=1), full], axis=0)
    return jnp.where(core == 0, zero, one)


def sum_body(me, g_ref, own_ref, other_ref):
    base = pl.program_id(0) * SUM_Z
    refs = (own_ref, other_ref) if me == 0 else (other_ref, own_ref)
    for z in range(SUM_Z):
        for pair in range(X // 2):
            at = (z * X + 2 * pair) * GROUP
            v = g_ref[0, at : at + 2 * GROUP, :].astype(F32)
            for m in range(1, g_ref.shape[0]):
                v = v + g_ref[m, at : at + 2 * GROUP, :].astype(F32)
            for k in range(2):
                first, both, last = [v[k * GROUP + j : k * GROUP + j + 8] for j in (0, 8, 16)]
                for core, owned in ((0, first), (1, last)):
                    o = refs[core].at[2 * pair + k, base + z]
                    o[0:8] = owned[:, :PC]
                    o[8:16] = owned[:, PC:]
                    o[16:24] = shared_tile(core, both[:, :PC], both[:, PC:])


def sum_kernel(*refs):
    me = lax.axis_index("c")
    for k in range(C):
        pl.when(me == k)(lambda k=k: sum_body(k, *refs))


def micro_sum(local):
    rows = SUM_Z * X * GROUP
    return pl.pallas_call(
        sum_kernel,
        out_shape=(pltpu.VMEM((X, Z, PR, PC), F32),) * 2,
        grid=(Z // SUM_Z,),
        in_specs=[pl.BlockSpec((local.shape[0], rows, COLS), lambda i: (0, i, 0))],
        out_specs=(pl.BlockSpec(memory_space=pltpu.VMEM),) * 2,
        name="micro_sum",
    )(local)


def adam(scale, total, master, moment1, moment2):
    clipped = scale * total
    m1 = BETA_ONE * moment1 + (1.0 - BETA_ONE) * clipped
    m2 = BETA_TWO * moment2 + (1.0 - BETA_TWO) * clipped * clipped
    first_hat = m1 / (1.0 - BETA_ONE**STEP)
    second_hat = m2 / (1.0 - BETA_TWO**STEP)
    new = master - LEARN_RATE * (
        first_hat / (jnp.sqrt(second_hat) + 1e-08) + DECAY_WEIGHT * master
    )
    return new, m1, m2


def update_kernel(elements, sq_ref, t_ref, ma_ref, m1_ref, m2_ref, em_ref, oma, om1, om2, oem, ow):
    core = lax.axis_index("c")
    sq = jnp.sum(jnp.sum(sq_ref[...], axis=0))
    sq = jnp.full((1, COLS), sq, F32)
    scale = jnp.minimum(1.0, 1.0 / jnp.sqrt(sq / elements + 1e-06))
    new, m1, m2 = adam(scale, from_piece(core, t_ref[...]), ma_ref[...], m1_ref[...], m2_ref[...])
    oma[...] = new
    om1[...] = m1
    om2[...] = m2
    oem[...] = EMA_KEEP * em_ref[...] + (1.0 - EMA_KEEP) * new
    ow[...] = jnp.broadcast_to(to_piece(core, new).astype(BF16)[None], ow.shape)


def place_kernel(w_ref, o_ref):
    base = pl.program_id(0) * NZ
    for z in range(NZ):
        for x in range(X):
            at = (z * X + x) * GROUP
            a, b = w_ref.at[0, x, base + z], w_ref.at[1, x, base + z]
            o_ref[at : at + 8, :PC] = a[0:8]
            o_ref[at : at + 8, PC:] = a[8:16]
            o_ref[at + 16 : at + 24, :PC] = b[0:8]
            o_ref[at + 16 : at + 24, PC:] = b[8:16]
            p, q = a[16:24].astype(F32), b[16:24].astype(F32)
            left = jnp.where(upper(), p, q)
            right = pltpu.roll(jnp.where(upper(), q, p), 4, 0)
            o_ref[at + 8 : at + 16, :PC] = left.astype(BF16)
            o_ref[at + 8 : at + 16, PC:] = right.astype(BF16)


def place(w):
    rows = NZ * X * GROUP
    return pl.pallas_call(
        place_kernel,
        out_shape=jax.ShapeDtypeStruct((STEPS * rows, COLS), BF16),
        grid=(STEPS,),
        in_specs=[pl.BlockSpec(memory_space=pltpu.VMEM)],
        out_specs=pl.BlockSpec((rows, COLS), lambda i: (i, 0)),
        name="place",
    )(*near(w))


def exchange(v, axes):
    return lax.all_to_all(v, axes, split_axis=0, concat_axis=0, tiled=True)


def near(*arrays):
    return [pltpu.with_memory_space_constraint(v, pltpu.VMEM) for v in arrays]


def copies(v, n):
    return jnp.broadcast_to(v[None], (n,) + v.shape)


def shards(grads, master, moment1, moment2, ema):
    local = grads[0]
    elements = local.shape[1] * local.shape[2] * T

    part, other = micro_sum(local)
    part = part + lax.ppermute(other, "c", [(0, 1), (1, 0)])
    part = exchange((part * LIFT).astype(F16), "x")
    part = jnp.sum(part.astype(F32), axis=0) * (1.0 / LIFT)
    total = jnp.sum(exchange(part, "z"), axis=0)
    sq = jnp.sum(total * total, axis=0, keepdims=True)
    sq = jnp.sum(exchange(copies(sq, X * C * T), ("x", "c", "t")), axis=0)
    sq = exchange(copies(sq, Z), "z")

    state = jax.ShapeDtypeStruct((ROWS, COLS), F32)
    whole = pl.BlockSpec(memory_space=pltpu.VMEM)
    new_master, new_moment1, new_moment2, new_ema, w = pl.pallas_call(
        lambda *refs: update_kernel(elements, *refs),
        out_shape=(state, state, state, state, pltpu.VMEM((Z, PR, PC), BF16)),
        in_specs=[whole] * 6,
        out_specs=(pl.BlockSpec(),) * 4 + (whole,),
        name="update",
    )(*near(sq, total, master, moment1, moment2, ema))

    w = exchange(w, "z")
    w = exchange(copies(w, X), "x")
    w = lax.all_gather(w, "c", axis=0, tiled=False)
    weights = place(w)
    return (new_master, new_moment1, new_moment2, new_ema, weights)


def solution(mesh):
    fine = Mesh(mesh.devices.reshape(Z, X, C, T), ("z", "x", "c", "t"))
    rows = ("z", "x", "c")
    return jax.shard_map(
        shards,
        mesh=fine,
        in_specs=(P(rows, None, None, "t"),) + (P(rows, "t"),) * 4,
        out_specs=(P(rows, "t"),) * 4 + (P(None, "t"),),
        check_vma=False,
    )
```
